32 devices in a mesh: patch: 16 (over z, y, x), grp: 2 (over core).
Axes of the slice: x: 2, y: 2, z: 4, core: 2. Of those that a mesh axis runs over, the one named last changes fastest.
Arguments:
- node_latent: float32 [5120, 512], P(('patch', 'grp')), may hold values from -6 to 6
- edge_latent: float32 [32768, 512], P(('patch', 'grp')), may hold values from -6 to 6
- node_cot: float32 [5120, 512], P(('patch', 'grp')), may hold values from -6 to 6
- edge_cot: float32 [32768, 512], P(('patch', 'grp')), may hold values from -6 to 6
- edge_w1: bfloat16 [1536, 512], replicated, may hold values from -0.15625 to 0.15625
- edge_w2: bfloat16 [512, 512], replicated, may hold values from -0.25 to 0.25
- edge_gain: float32 [512], replicated, may hold values from 0.1 to 1.9
- node_w1: bfloat16 [1024, 512], replicated, may hold values from -0.1875 to 0.1875
- node_w2: bfloat16 [512, 512], replicated, may hold values from -0.25 to 0.25
- node_gain: float32 [512], replicated, may hold values from 0.1 to 1.9
- senders: int32 [32768], P(('patch', 'grp')), may hold values from 0 to 959, as said below
- receivers: int32 [32768], P(('patch', 'grp')), may hold values from 0 to 319
- counts: int32 [32], P(('patch', 'grp')), may hold values from 256 to 1024, as said below
Outputs:
- node_grad: float32 [5120, 512], P(('patch', 'grp'))
- edge_grad: float32 [32768, 512], P(('patch', 'grp'))
- grad_edge_w1: float32 [1536, 512], P('grp')
- grad_edge_w2: float32 [512, 512], P('grp')
- grad_node_w1: float32 [1024, 512], P('grp')
- grad_node_w2: float32 [512, 512], P('grp')
The draws below stay inside these ranges and needn't reach their ends.
Inputs may be any that keep to these rules, and one draw needn't show every extreme that they name: `senders`: indices into the nodes of the previous patch, the own patch and the next patch (patches taken cyclically), 320 rows each, in that order. `counts`: each device's live edges fill its first slots; some device is full in every draw.
All inputs are finite; a program needn't handle non-finite values.
Results may differ from the reference program's by a relative error of at most 0.0068.
Values may be sent and summed in bfloat16 or wider, within the bound.
A program may use at most 128 MiB of HBM per device.

```python
import math
import jax
import jax.numpy as jnp
import numpy as np
from jax import lax

D = 512
EDGE_DEV = 1024
NODE_PATCH = 320
NODES = 5120
EDGES = 32768
N_PATCH = 16
N_GRP = 2
DEVICES = 32


def draw_senders(key, part):
    first, second = jax.random.split(jax.random.fold_in(key, 11))
    pick = jax.random.randint(first, (EDGES,), 0, 5)
    slab = jnp.where(pick == 0, 0, jnp.where(pick == 4, 2, 1))
    within = jax.random.randint(second, (EDGES,), 0, NODE_PATCH)
    return (slab * NODE_PATCH + within).astype(jnp.int32)


def draw_counts(key, part):
    first, second = jax.random.split(jax.random.fold_in(key, 23))
    level = jax.random.randint(first, (DEVICES,), 0, 65)
    base = EDGE_DEV // 4 + 3 * EDGE_DEV // 4 * level * level // 4096
    full = jax.random.randint(second, (), 0, DEVICES)
    return jnp.where(jnp.arange(DEVICES) == full, EDGE_DEV, base).astype(jnp.int32)


def touch_ends(drawn, rng, least, top_value):
    longest = drawn.shape.index(max(drawn.shape))
    spots = []
    for shift in (0, 1):
        where = [jax.random.randint(jax.random.fold_in(rng, axis), (), 0, length) for axis, length in enumerate(drawn.shape)]
        where[longest] = (where[longest] + shift) % drawn.shape[longest]
        spots.append(tuple(where))
    return drawn.at[spots[0]].set(least).at[spots[1]].set(top_value)


def steps_of(own_key, dims, cuts, smallest, largest):
    level = 1.0
    for axis_at, shards_of in cuts:
        heights = jax.random.uniform(jax.random.fold_in(jax.random.fold_in(own_key, 6), axis_at), (shards_of,), jnp.float32, smallest / len(cuts), largest / len(cuts))
        level = level * jnp.repeat(jnp.exp(heights), dims[axis_at] // shards_of).reshape((-1,) + (1,) * (len(dims) - 1 - axis_at))
    return level


def rank_table(number_of, skew):
    weights = [(1 << 20) // math.isqrt(standing ** skew) + 1 for standing in range(1, number_of + 1)]
    deviation = 1 + sum(weights) // (1 << 30)
    return np.cumsum(np.array([max(1, weight // deviation) for weight in weights]))


def ranked(rng, dims, amount, slope):
    grid = rank_table(amount, slope)
    lot = jax.random.randint(jax.random.fold_in(rng, 1), dims, 0, int(grid[amount - 1]))
    grade = jnp.searchsorted(jnp.asarray(grid, jnp.int32), lot, side="right")
    return jax.random.permutation(jax.random.fold_in(rng, 2), amount)[grade].astype(jnp.int32)


def noise(key, extent, width, limit, cuts=(), held_as=jnp.bfloat16):
    array = width * jax.random.normal(key, extent, jnp.float32)
    if cuts:
        array = array * steps_of(key, extent, cuts, -0.22, 0.18)
    return jnp.clip(array, -limit, limit).astype(held_as)


def setup_inputs(seed: int = 0) -> dict:
    keys = jax.random.split(jax.random.key(seed), 14)
    return {
        "node_latent": noise(keys[0], (NODES, D), 1.0, 6.0, ((0, 32),), jnp.float32),
        "edge_latent": noise(keys[1], (EDGES, D), 1.0, 6.0, ((0, 32),), jnp.float32),
        "node_cot": noise(keys[2], (NODES, D), 1.0, 6.0, ((0, 32),), jnp.float32),
        "edge_cot": noise(keys[3], (EDGES, D), 1.0, 6.0, ((0, 32),), jnp.float32),
        "edge_w1": noise(keys[4], (3 * D, D), (3 * D) ** -0.5, 0.15625),
        "edge_w2": noise(keys[5], (D, D), D ** -0.5, 0.25),
        "edge_gain": jnp.clip(1.0 + 0.18 * jax.random.normal(keys[6], (D,), jnp.float32), 0.1, 1.9),
        "node_w1": noise(keys[7], (2 * D, D), (2 * D) ** -0.5, 0.1875),
        "node_w2": noise(keys[8], (D, D), D ** -0.5, 0.25),
        "node_gain": jnp.clip(1.0 + 0.18 * jax.random.normal(keys[9], (D,), jnp.float32), 0.1, 1.9),
        "senders": draw_senders(jax.random.fold_in(keys[13], 71), 0),
        "receivers": touch_ends(ranked(keys[11], (EDGES,), NODE_PATCH, 1), jax.random.fold_in(keys[11], 3), 0, NODE_PATCH - 1).astype(jnp.int32),
        "counts": draw_counts(jax.random.fold_in(keys[13], 71), 0),
    }


EPS = 1e-05

def silu_grad(pre):
    sig = jax.nn.sigmoid(pre)
    return sig * (1.0 + pre * (1.0 - sig))

def norm_forward(out, gain):
    center = out - lax.optimization_barrier(jnp.mean(out, axis=-1, keepdims=True))
    inv_std = lax.rsqrt(lax.optimization_barrier(jnp.mean(center * center, axis=-1, keepdims=True)) + EPS)
    normed = center * inv_std
    return (normed * gain, normed, inv_std)

def norm_backward(grad_y, gain, normed, inv_std):
    scaled = grad_y * gain
    return inv_std * (scaled - lax.optimization_barrier(jnp.mean(scaled, axis=-1, keepdims=True)) - normed * lax.optimization_barrier(jnp.mean(scaled * normed, axis=-1, keepdims=True)))

def mlp_forward(inputs, first, second, gain):
    pre = jnp.dot(inputs, first, preferred_element_type=jnp.float32)
    act = jax.nn.silu(pre).astype(jnp.bfloat16)
    out = jnp.dot(act, second, preferred_element_type=jnp.float32)
    upd, normed, inv_std = norm_forward(out, gain)
    return (upd, pre, act, normed, inv_std)

def mlp_backward(grad_y, inputs, first, second, gain, pre, act, normed, inv_std):
    grad_out = norm_backward(grad_y, gain, normed, inv_std).astype(jnp.bfloat16)
    grad_second = jnp.dot(act.T, grad_out, preferred_element_type=jnp.float32)
    grad_act = jnp.dot(grad_out, second.T, preferred_element_type=jnp.float32)
    grad_pre = (grad_act * silu_grad(pre)).astype(jnp.bfloat16)
    grad_first = jnp.dot(inputs.T, grad_pre, preferred_element_type=jnp.float32)
    grad_in = jnp.dot(grad_pre, first.T, preferred_element_type=jnp.float32)
    return (grad_in, grad_first, grad_second)

def reference(node_latent, edge_latent, node_cot, edge_cot, edge_w1, edge_w2, edge_gain, node_w1, node_w2, node_gain, senders, receivers, counts):
    slots = jnp.arange(EDGES, dtype=jnp.int32)
    device = slots // EDGE_DEV
    patch_of = device // N_GRP
    live = (slots % EDGE_DEV < counts[device]).astype(jnp.float32)[:, None]
    recv_node = (patch_of * NODE_PATCH + receivers).astype(jnp.int32)
    slab = senders // NODE_PATCH
    send_node = ((patch_of + slab - 1) % N_PATCH * NODE_PATCH + senders % NODE_PATCH).astype(jnp.int32)
    node_bf = node_latent.astype(jnp.bfloat16)
    edge_in = jnp.concatenate([edge_latent.astype(jnp.bfloat16), node_bf[send_node], node_bf[recv_node]], axis=1)
    edge_upd, edge_pre, edge_act, edge_normed, edge_inv = mlp_forward(edge_in, edge_w1, edge_w2, edge_gain)
    edge_upd = edge_upd * live
    aggregate = jax.ops.segment_sum(edge_upd, recv_node, num_segments=NODES)
    node_in = jnp.concatenate([node_bf, aggregate.astype(jnp.bfloat16)], axis=1)
    node_upd, node_pre, node_act, node_normed, node_inv = mlp_forward(node_in, node_w1, node_w2, node_gain)
    node_gin, grad_node_w1, grad_node_w2 = mlp_backward(node_cot, node_in, node_w1, node_w2, node_gain, node_pre, node_act, node_normed, node_inv)
    grad_agg = node_gin[:, D:]
    edge_gupd = (edge_cot + grad_agg[recv_node]) * live
    edge_gin, grad_edge_w1, grad_edge_w2 = mlp_backward(edge_gupd, edge_in, edge_w1, edge_w2, edge_gain, edge_pre, edge_act, edge_normed, edge_inv)
    edge_grad = edge_cot + edge_gin[:, :D]
    node_grad = node_cot + node_gin[:, :D]
    node_grad = node_grad + jax.ops.segment_sum(edge_gin[:, D:2 * D], send_node, num_segments=NODES)
    node_grad = node_grad + jax.ops.segment_sum(edge_gin[:, 2 * D:], recv_node, num_segments=NODES)
    return (node_grad, edge_grad, grad_edge_w1, grad_edge_w2, grad_node_w1, grad_node_w2)
```

```python
import functools

import jax
import jax.numpy as jnp
from jax import lax
from jax.experimental import pallas as pl
from jax.experimental.pallas import tpu as pltpu
from jax.sharding import PartitionSpec as P

EPS = 1e-05
BF = jnp.bfloat16
F32 = jnp.float32
MESH = pl.DeviceIdType.MESH
VMEM = pl.BlockSpec(memory_space=pltpu.VMEM)
SMEM = pl.BlockSpec(memory_space=pltpu.SMEM)
LIMIT = 60 * 1024 * 1024


def axis_sizes(n):
    x = round((n / 2) ** (1 / 3))
    return (x, x, 2 * x) if 2 * x**3 == n else (1, 1, n)


def dot(a, b):
    return jnp.dot(a, b, preferred_element_type=F32)


def dot_tn(a, b):
    return lax.dot_general(a, b, (((0,), (0,)), ((), ())), preferred_element_type=F32)


def dot_nt(a, b):
    return lax.dot_general(a, b, (((1,), (1,)), ((), ())), preferred_element_type=F32)


def hot_rows(col, width):
    at = lax.broadcasted_iota(jnp.int32, (col.shape[0], width), 1)
    return jnp.where(at == col, 1.0, 0.0).astype(BF)


def hot_cols(row, height):
    at = lax.broadcasted_iota(jnp.int32, (height, row.shape[1]), 0)
    return jnp.where(at == row, 1.0, 0.0).astype(BF)


def mean(x):
    return jnp.mean(x, axis=-1, keepdims=True)


def mlp_tail(pre, w2):
    sig = jax.nn.sigmoid(pre)
    act = (pre * sig).astype(BF)
    slope = sig * (1.0 + pre * (1.0 - sig))
    out = dot(act, w2)
    center = out - mean(out)
    inv = lax.rsqrt(mean(center * center) + EPS)
    return act, slope, center * inv, inv


def norm_backward(grad, gain, normed, inv):
    scaled = grad * gain
    return (inv * (scaled - mean(scaled) - normed * mean(scaled * normed))).astype(BF)


def greet(peers):
    barrier = pltpu.get_barrier_semaphore()
    for peer in peers:
        pl.semaphore_signal(barrier, inc=1, device_id=peer, device_id_type=MESH)
    pl.semaphore_wait(barrier, len(peers))


def remote(src, dst, send, recv, device):
    return pltpu.make_async_remote_copy(
        src_ref=src, dst_ref=dst, send_sem=send, recv_sem=recv, device_id=device, device_id_type=MESH
    )


def comm_params(ident):
    return pltpu.CompilerParams(collective_id=ident, has_side_effects=True, vmem_limit_bytes=LIMIT)


def exchange_kernel(n, x_ref, ext_ref, send, recv, local):
    rows = x_ref.shape[0]
    p, g = lax.axis_index("patch"), lax.axis_index("grp")
    after, before = lax.rem(p + 1, n), lax.rem(p + n - 1, n)
    mate = (p, 1 - g)
    greet([mate, (after, g), (before, g)])

    def place(slab):
        return ext_ref.at[slab, g]

    own = pltpu.make_async_copy(x_ref, place(1), local)
    to_after = remote(x_ref, place(0), send.at[0], recv.at[0], (after, g))
    to_before = remote(x_ref, place(2), send.at[1], recv.at[1], (before, g))
    to_mate = remote(x_ref, place(1), send.at[2], recv.at[2], mate)
    to_after.start()
    to_before.start()
    to_mate.start()
    own.start()
    to_after.wait_recv()
    pass_0 = remote(place(0), place(0), send.at[3], recv.at[3], mate)
    pass_0.start()
    to_before.wait_recv()
    pass_2 = remote(place(2), place(2), send.at[4], recv.at[4], mate)
    pass_2.start()
    own.wait()
    to_mate.wait()
    pass_0.wait()
    pass_2.wait()
    to_after.wait_send()
    to_before.wait_send()


def exchange(node_bf, n):
    rows, d = node_bf.shape
    return pl.pallas_call(
        functools.partial(exchange_kernel, n),
        out_shape=jax.ShapeDtypeStruct((3, 2, rows, d), BF),
        in_specs=[VMEM],
        out_specs=VMEM,
        scratch_shapes=[
            pltpu.SemaphoreType.DMA((5,)),
            pltpu.SemaphoreType.DMA((5,)),
            pltpu.SemaphoreType.DMA,
        ],
        compiler_params=comm_params(0),
        name="node_exchange",
    )(node_bf)


def forward_kernel(
    count, el, ext, snd_c, rcv_c, rcv_r, w1, w2, gain, act_o, slope_o, normed_o, inv_o, agg_o, agg
):
    i = pl.program_id(0)
    tile, d = el.shape
    nodes = agg.shape[0]
    x_s = dot(hot_rows(snd_c[...], 3 * nodes), ext[...]).astype(BF)
    x_r = dot(hot_rows(rcv_c[...], nodes), ext[nodes : 2 * nodes, :]).astype(BF)
    pre = dot(el[...].astype(BF), w1[0:d, :])
    pre += dot(x_s, w1[d : 2 * d, :])
    pre += dot(x_r, w1[2 * d : 3 * d, :])
    act, slope, normed, inv = mlp_tail(pre, w2[...])
    act_o[...] = act
    slope_o[...] = slope.astype(BF)
    normed_o[...] = normed.astype(BF)
    inv_o[...] = inv
    slot = i * tile + lax.broadcasted_iota(jnp.int32, (tile, 1), 0)
    upd = jnp.where(slot < count[0], normed * gain[...], 0.0).astype(BF)
    part = dot(hot_cols(rcv_r[...], nodes), upd)

    @pl.when(i == 0)
    def _():
        agg[...] = part

    @pl.when(i > 0)
    def _():
        agg[...] += part

    @pl.when(i == pl.num_programs(0) - 1)
    def _():
        agg_o[...] = agg[...].astype(BF)


def whole(shape):
    return pl.BlockSpec(shape, lambda i: (0, 0), pipeline_mode=pl.Buffered(1))


def edge_forward(count, el, ext, snd_c, rcv_c, rcv_r, w1, w2, gain, tiles):
    edges, d = el.shape
    nodes = ext.shape[0] // 3
    tile = edges // tiles

    def rows(width):
        return pl.BlockSpec((tile, width), lambda i: (i, 0))

    return pl.pallas_call(
        forward_kernel,
        grid=(tiles,),
        out_shape=(
            jax.ShapeDtypeStruct((edges, d), BF),
            jax.ShapeDtypeStruct((edges, d), BF),
            jax.ShapeDtypeStruct((edges, d), BF),
            jax.ShapeDtypeStruct((edges, 1), F32),
            jax.ShapeDtypeStruct((nodes, d), BF),
        ),
        in_specs=[
            SMEM,
            rows(d),
            whole(ext.shape),
            rows(1),
            rows(1),
            pl.BlockSpec((1, tile), lambda i: (0, i)),
            whole(w1.shape),
            whole(w2.shape),
            whole(gain.shape),
        ],
        out_specs=(rows(d), rows(d), rows(d), rows(1), whole((nodes, d))),
        scratch_shapes=[pltpu.VMEM((nodes, d), F32)],
        compiler_params=pltpu.CompilerParams(
            dimension_semantics=("arbitrary",), vmem_limit_bytes=LIMIT
        ),
        name="edge_forward",
    )(count, el, ext, snd_c, rcv_c, rcv_r, w1, w2, gain)


def node_kernel(
    agg, lat, cot, w1, w2, gain, gagg_o, part_o, dw1_o, dw2_o, other, mine, send, recv, local
):
    p, g = lax.axis_index("patch"), lax.axis_index("grp")
    mate = (p, 1 - g)
    d = lat.shape[1]
    greet([mate])
    swap = remote(agg.at[1 - g], other, send.at[0], recv.at[0], mate)
    swap.start()
    lat_bf = lat[...].astype(BF)
    pre = dot(lat_bf, w1[0:d, :])
    swap.wait()
    agg_bf = (agg[g].astype(F32) + other[...].astype(F32)).astype(BF)
    pre += dot(agg_bf, w1[d : 2 * d, :])
    act, slope, normed, inv = mlp_tail(pre, w2[...])
    gout = norm_backward(cot[...], gain[...], normed, inv)
    gpre = (dot_nt(gout, w2[...]) * slope).astype(BF)
    mine[...] = dot_nt(gpre, w1[d : 2 * d, :]).astype(BF)
    keep = pltpu.make_async_copy(mine, gagg_o.at[g], local)
    keep.start()
    give = remote(mine, gagg_o.at[g], send.at[1], recv.at[1], mate)
    give.start()
    part_o[...] = cot[...] + dot_nt(gpre, w1[0:d, :])
    dw2_o[...] = dot_tn(act, gout).astype(BF)
    dw1_o[0:d, :] = dot_tn(lat_bf, gpre).astype(BF)
    dw1_o[d : 2 * d, :] = dot_tn(agg_bf, gpre).astype(BF)
    keep.wait()
    give.wait()


def node_layer(agg, lat, cot, w1, w2, gain):
    rows, d = lat.shape
    return pl.pallas_call(
        node_kernel,
        out_shape=(
            jax.ShapeDtypeStruct((2, rows, d), BF),
            jax.ShapeDtypeStruct((rows, d), F32),
            jax.ShapeDtypeStruct(w1.shape, BF),
            jax.ShapeDtypeStruct(w2.shape, BF),
        ),
        in_specs=[VMEM] * 6,
        out_specs=(VMEM,) * 4,
        scratch_shapes=[
            pltpu.VMEM((rows, d), BF),
            pltpu.VMEM((rows, d), BF),
            pltpu.SemaphoreType.DMA((2,)),
            pltpu.SemaphoreType.DMA((2,)),
            pltpu.SemaphoreType.DMA,
        ],
        compiler_params=comm_params(1),
        name="node_layer",
    )(agg, lat, cot, w1, w2, gain)


def backward_kernel(
    count, el, ec, act, slope, normed, inv, gagg, ext, snd_r, rcv_c, rcv_r, w1, w2, gain,
    grad_o, sent_o, dw1_o, dw2_o, by_s, by_r, dwe, dw2,
):
    i = pl.program_id(0)
    tile, d = el.shape
    nodes = gagg.shape[0]

    @pl.when(i == 0)
    def _():
        by_s[...] = jnp.zeros_like(by_s)
        by_r[...] = jnp.zeros_like(by_r)
        dwe[...] = jnp.zeros_like(dwe)
        dw2[...] = jnp.zeros_like(dw2)

    slot = i * tile + lax.broadcasted_iota(jnp.int32, (tile, 1), 0)
    back = dot(hot_rows(rcv_c[...], nodes), gagg[...])
    gupd = jnp.where(slot < count[0], ec[...] + back, 0.0)
    gout = norm_backward(gupd, gain[...], normed[...].astype(F32), inv[...])
    gpre = (dot_nt(gout, w2[...]) * slope[...].astype(F32)).astype(BF)
    grad_o[...] = ec[...] + dot_nt(gpre, w1[0:d, :])
    dw2[...] += dot_tn(act[...], gout)
    dwe[...] += dot_tn(el[...].astype(BF), gpre)
    by_s[...] += dot(hot_cols(snd_r[...], 3 * nodes), gpre)
    by_r[...] += dot(hot_cols(rcv_r[...], nodes), gpre)

    @pl.when(i == pl.num_programs(0) - 1)
    def _():
        dw2_o[...] = dw2[...].astype(BF)
        dw1_o[0:d, :] = dwe[...].astype(BF)
        s_bf = by_s[...].astype(BF)
        r_bf = by_r[...].astype(BF)
        dw1_o[d : 2 * d, :] = dot_tn(ext[...], s_bf).astype(BF)
        dw1_o[2 * d : 3 * d, :] = dot_tn(ext[nodes : 2 * nodes, :], r_bf).astype(BF)
        spread = dot_nt(s_bf, w1[d : 2 * d, :])
        sent_o[0:nodes, :] = spread[0:nodes].astype(BF)
        kept = spread[nodes : 2 * nodes] + dot_nt(r_bf, w1[2 * d : 3 * d, :])
        sent_o[nodes : 2 * nodes, :] = kept.astype(BF)
        sent_o[2 * nodes : 3 * nodes, :] = spread[2 * nodes : 3 * nodes].astype(BF)


def edge_backward(
    count, el, ec, act, slope, normed, inv, gagg, ext, snd_r, rcv_c, rcv_r, w1, w2, gain, tiles
):
    edges, d = el.shape
    nodes = gagg.shape[0]
    tile = edges // tiles

    def rows(width):
        return pl.BlockSpec((tile, width), lambda i: (i, 0))

    line = pl.BlockSpec((1, tile), lambda i: (0, i))
    return pl.pallas_call(
        backward_kernel,
        grid=(tiles,),
        out_shape=(
            jax.ShapeDtypeStruct((edges, d), F32),
            jax.ShapeDtypeStruct((3 * nodes, d), BF),
            jax.ShapeDtypeStruct(w1.shape, BF),
            jax.ShapeDtypeStruct(w2.shape, BF),
        ),
        in_specs=[
            SMEM, rows(d), rows(d), rows(d), rows(d), rows(d), rows(1),
            whole(gagg.shape), whole(ext.shape), line, rows(1), line,
            whole(w1.shape), whole(w2.shape), whole(gain.shape),
        ],
        out_specs=(rows(d), whole((3 * nodes, d)), whole(w1.shape), whole(w2.shape)),
        scratch_shapes=[
            pltpu.VMEM((3 * nodes, d), F32),
            pltpu.VMEM((nodes, d), F32),
            pltpu.VMEM((d, d), F32),
            pltpu.VMEM((d, d), F32),
        ],
        compiler_params=pltpu.CompilerParams(
            dimension_semantics=("arbitrary",), vmem_limit_bytes=LIMIT
        ),
        name="edge_backward",
    )(count, el, ec, act, slope, normed, inv, gagg, ext, snd_r, rcv_c, rcv_r, w1, w2, gain)


def plan_of(rows, sizes, order):
    steps = []
    for axis in order:
        n = sizes[axis]
        if n > 1:
            left = rows // n if rows % (16 * n) == 0 else rows
            steps.append((axis, n, rows, left))
            rows = left
    return steps


def reduce_kernel(n, plans, widths, names, *refs):
    sent, d_e1, d_e2, d_n1, d_n2, share_o = refs[:6]
    outs = refs[6:8]
    rest = dict(zip(names, refs[8:]))
    p, g = lax.axis_index("patch"), lax.axis_index("grp")
    nx, ny, nz = axis_sizes(n)
    here = (lax.rem(p, nx), lax.rem(p // nx, ny), p // (nx * ny))
    sizes, strides = (nx, ny, nz), (1, nx, nx * ny)
    after, before = lax.rem(p + 1, n), lax.rem(p + n - 1, n)
    mate = (p, 1 - g)

    def along(axis, step):
        c = here[axis]
        t = lax.rem(c + step, sizes[axis])
        return t, (p + (t - c) * strides[axis], g)

    peers = [mate, (after, g), (before, g)]
    for axis in range(3):
        peers += [along(axis, step)[1] for step in range(1, sizes[axis])]
    greet(peers)
    send, recv = rest["send"], rest["recv"]
    used = [0]
    pending = []

    def go(src, dst, device):
        k = used[0]
        used[0] += 1
        copy = remote(src, dst, send.at[k], recv.at[k], device)
        copy.start()
        pending.append(copy)
        return copy

    def window(ref, start, size, cols):
        if not isinstance(start, int):
            start = pl.multiple_of(start, 16)
        return ref.at[pl.ds(start, size), cols]

    halves = ((d_n1, d_n2), (d_e2, d_e1))
    first = []
    for s in range(2):
        got, at = [], 0
        for part in halves[s]:
            size = part.shape[1]
            got.append((go(part.at[1 - g], rest[f"in{s}"].at[pl.ds(at, size)], mate), part, at, size))
            at += size
        first.append(got)
        if s == 0:
            nodes_in = [go(sent.at[k, 1 - g], rest["sin"].at[k], mate) for k in range(3)]

    def start_reduce(s, c, k):
        axis, m, r, left = plans[s][c][k]
        cols = pl.ds(c * widths, widths)
        flow = []
        for step in range(1, m):
            t, device = along(axis, step)
            if k == 0:
                base = rest[f"cur{s}"]
                src = window(base, t * left if left < r else 0, left, cols)
            else:
                base = rest[f"acc{s}_{c}_{k - 1}"]
                src = window(base, t * left if left < r else 0, left, pl.ds(0, widths))
            flow.append(go(src, rest[f"rx{s}_{c}_{k}"].at[step - 1], device))
        return flow

    def finish_reduce(s, c, k, flow):
        axis, m, r, left = plans[s][c][k]
        mine = here[axis] * left if left < r else 0
        for copy in flow:
            copy.wait_recv()
        if k == 0:
            own = window(rest[f"cur{s}"], mine, left, pl.ds(c * widths, widths))
        else:
            own = window(rest[f"acc{s}_{c}_{k - 1}"], mine, left, pl.ds(0, widths))
        total = own[...].astype(F32)
        for step in range(m - 1):
            total += rest[f"rx{s}_{c}_{k}"][step].astype(F32)
        return total.astype(BF)

    def offset(s, c, depth):
        at = 0
        for axis, m, r, left in plans[s][c][:depth]:
            if left < r:
                at = at + here[axis] * left
        return at

    def start_gather(s, c, k):
        axis, m, r, left = plans[s][c][k]
        if left == r:
            return []
        cols = pl.ds(c * widths, widths)
        block = window(outs[s], offset(s, c, k + 1), left, cols)
        return [go(block, block, along(axis, step)[1]) for step in range(1, m)]

    flows = {}
    depth = len(plans[0][0])
    for s in range(2):
        cur = rest[f"cur{s}"]
        for copy, part, at, size in first[s]:
            copy.wait_recv()
            cur[at : at + size, :] = (
                part[g].astype(F32) + rest[f"in{s}"][at : at + size, :].astype(F32)
            ).astype(BF)
        for c in range(2):
            flows[s, c] = start_reduce(s, c, 0)
        if s == 0:
            for copy in nodes_in:
                copy.wait_recv()
            home = rest["home"]
            total = sent[:, g].astype(F32) + rest["sin"][...].astype(F32)
            home[...] = total.astype(BF)
            share = total[1]
            back = go(home.at[0], rest["from"].at[0], (before, g))
            forth = go(home.at[2], rest["from"].at[1], (after, g))
    for k in range(depth):
        for s in range(2):
            for c in range(2):
                total = finish_reduce(s, c, k, flows[s, c])
                if k < depth - 1:
                    rest[f"acc{s}_{c}_{k}"][...] = total
                    flows[s, c] = start_reduce(s, c, k + 1)
                else:
                    block = window(
                        outs[s], offset(s, c, depth), plans[s][c][k][3], pl.ds(c * widths, widths)
                    )
                    block[...] = total
                    flows[s, c] = start_gather(s, c, k)
    back.wait_recv()
    forth.wait_recv()
    share_o[...] = (
        rest["home"][1].astype(F32) + rest["from"][0].astype(F32) + rest["from"][1].astype(F32)
    )
    for k in range(depth - 1, -1, -1):
        for s in range(2):
            for c in range(2):
                for copy in flows[s, c]:
                    copy.wait_recv()
                if k > 0:
                    flows[s, c] = start_gather(s, c, k - 1)
    for copy in pending:
        copy.wait_send()


def reduce_all(n, sent, d_e1, d_e2, d_n1, d_n2):
    d = sent.shape[-1]
    rows = sent.shape[2]
    sizes = axis_sizes(n)
    totals = (d_n1.shape[1] + d_n2.shape[1], d_e2.shape[1] + d_e1.shape[1])
    orders = ((0, 1, 2), (1, 0, 2))
    plans = [[plan_of(total, sizes, order) for order in orders] for total in totals]
    wide = d // 2
    scratch = {
        "sin": pltpu.VMEM((3, rows, d), BF),
        "home": pltpu.VMEM((3, rows, d), BF),
        "from": pltpu.VMEM((2, rows, d), BF),
    }
    copies = 4 + 3 + 2
    for s in range(2):
        scratch[f"in{s}"] = pltpu.VMEM((totals[s], d), BF)
        scratch[f"cur{s}"] = pltpu.VMEM((totals[s], d), BF)
        for c in range(2):
            for k, (axis, m, r, left) in enumerate(plans[s][c]):
                scratch[f"rx{s}_{c}_{k}"] = pltpu.VMEM((m - 1, left, wide), BF)
                scratch[f"acc{s}_{c}_{k}"] = pltpu.VMEM((left, wide), BF)
                copies += 2 * (m - 1)
    scratch["send"] = pltpu.SemaphoreType.DMA((copies,))
    scratch["recv"] = pltpu.SemaphoreType.DMA((copies,))
    return pl.pallas_call(
        functools.partial(reduce_kernel, n, plans, wide, tuple(scratch)),
        out_shape=(
            jax.ShapeDtypeStruct((rows, d), F32),
            jax.ShapeDtypeStruct((totals[0], d), BF),
            jax.ShapeDtypeStruct((totals[1], d), BF),
        ),
        in_specs=[VMEM] * 5,
        out_specs=(VMEM,) * 3,
        scratch_shapes=list(scratch.values()),
        compiler_params=comm_params(2),
        name="reduce_all",
    )(sent, d_e1, d_e2, d_n1, d_n2)


def local(
    node_latent,
    edge_latent,
    node_cot,
    edge_cot,
    edge_w1,
    edge_w2,
    edge_gain,
    node_w1,
    node_w2,
    node_gain,
    senders,
    receivers,
    counts,
):
    n = lax.axis_size("patch")
    rows, d = node_latent.shape
    edges = edge_latent.shape[0]
    tiles = 4
    ext = exchange(node_latent.astype(BF), n).reshape(6 * rows, d)
    snd_c, rcv_c = senders.reshape(edges, 1), receivers.reshape(edges, 1)
    snd_r, rcv_r = senders.reshape(1, edges), receivers.reshape(1, edges)
    e_gain, n_gain = edge_gain.reshape(1, d), node_gain.reshape(1, d)
    act, slope, normed, inv, agg = edge_forward(
        counts, edge_latent, ext, snd_c, rcv_c, rcv_r, edge_w1, edge_w2, e_gain, tiles
    )
    gagg, part, d_n1, d_n2 = node_layer(
        agg.reshape(2, rows, d), node_latent, node_cot, node_w1, node_w2, n_gain
    )
    edge_grad, sent, d_e1, d_e2 = edge_backward(
        counts, edge_latent, edge_cot, act, slope, normed, inv, gagg.reshape(2 * rows, d), ext,
        snd_r, rcv_c, rcv_r, edge_w1, edge_w2, e_gain, tiles,
    )

    def halves(x):
        return x.reshape(2, x.shape[0] // 2, d)

    share, node_sum, edge_sum = reduce_all(
        n, sent.reshape(3, 2, rows, d), halves(d_e1), halves(d_e2), halves(d_n1), halves(d_n2)
    )
    cut_n, cut_e = node_w1.shape[0] // 2, edge_w2.shape[0] // 2
    return (
        part + share,
        edge_grad,
        edge_sum[cut_e:].astype(F32),
        edge_sum[:cut_e].astype(F32),
        node_sum[:cut_n].astype(F32),
        node_sum[cut_n:].astype(F32),
    )


def solution(mesh):
    line = P(("patch", "grp"))
    block = P(("patch", "grp"), None)
    in_specs = (block,) * 4 + (P(),) * 6 + (line,) * 3
    out_specs = (block, block) + (P("grp", None),) * 4
    return jax.shard_map(local, mesh=mesh, in_specs=in_specs, out_specs=out_specs, check_vma=False)
```

```python
import functools

import jax
import jax.numpy as jnp
from jax import lax
from jax.experimental import pallas as pl
from jax.experimental.pallas import tpu as pltpu
from jax.sharding import PartitionSpec as P

EPS = 1e-05
BF = jnp.bfloat16
F32 = jnp.float32
MESH = pl.DeviceIdType.MESH
VMEM = pl.BlockSpec(memory_space=pltpu.VMEM)
SMEM = pl.BlockSpec(memory_space=pltpu.SMEM)
LIMIT = 60 * 1024 * 1024


def axis_sizes(n):
    x = round((n / 2) ** (1 / 3))
    return (x, x, 2 * x) if 2 * x**3 == n else (1, 1, n)


def dot(a, b):
    return jnp.dot(a, b, preferred_element_type=F32)


def dot_tn(a, b):
    return lax.dot_general(a, b, (((0,), (0,)), ((), ())), preferred_element_type=F32)


def dot_nt(a, b):
    return lax.dot_general(a, b, (((1,), (1,)), ((), ())), preferred_element_type=F32)


def hot_rows(col, width):
    at = lax.broadcasted_iota(jnp.int32, (col.shape[0], width), 1)
    return jnp.where(at == col, 1.0, 0.0).astype(BF)


def hot_cols(row, height):
    at = lax.broadcasted_iota(jnp.int32, (height, row.shape[1]), 0)
    return jnp.where(at == row, 1.0, 0.0).astype(BF)


def column(row):
    return jnp.transpose(jnp.broadcast_to(row, (128, row.shape[1])))[:, 0:1]


def mean(x):
    return jnp.mean(x, axis=-1, keepdims=True)


def mlp_tail(pre, w2):
    sig = jax.nn.sigmoid(pre)
    act = (pre * sig).astype(BF)
    slope = sig * (1.0 + pre * (1.0 - sig))
    out = dot(act, w2)
    center = out - mean(out)
    inv = lax.rsqrt(mean(center * center) + EPS)
    return act, slope, center * inv, inv


def norm_backward(grad, gain, normed, inv):
    scaled = grad * gain
    return (inv * (scaled - mean(scaled) - normed * mean(scaled * normed))).astype(BF)


def greet(peers):
    barrier = pltpu.get_barrier_semaphore()
    for peer in peers:
        pl.semaphore_signal(barrier, inc=1, device_id=peer, device_id_type=MESH)
    pl.semaphore_wait(barrier, len(peers))


def remote(src, dst, send, recv, device):
    return pltpu.make_async_remote_copy(
        src_ref=src, dst_ref=dst, send_sem=send, recv_sem=recv, device_id=device, device_id_type=MESH
    )


def comm_params(ident):
    return pltpu.CompilerParams(collective_id=ident, has_side_effects=True, vmem_limit_bytes=LIMIT)


def exchange_kernel(n, lat_ref, ext_ref, x_ref, send, recv, local):
    x_ref[...] = lat_ref[...].astype(BF)
    p, g = lax.axis_index("patch"), lax.axis_index("grp")
    after, before = lax.rem(p + 1, n), lax.rem(p + n - 1, n)
    mate = (p, 1 - g)
    greet([mate, (after, g), (before, g)])

    def place(slab):
        return ext_ref.at[slab, g]

    own = pltpu.make_async_copy(x_ref, place(1), local)
    to_after = remote(x_ref, place(0), send.at[0], recv.at[0], (after, g))
    to_before = remote(x_ref, place(2), send.at[1], recv.at[1], (before, g))
    to_mate = remote(x_ref, place(1), send.at[2], recv.at[2], mate)
    to_after.start()
    to_before.start()
    to_mate.start()
    own.start()
    to_after.wait_recv()
    pass_0 = remote(place(0), place(0), send.at[3], recv.at[3], mate)
    pass_0.start()
    to_before.wait_recv()
    pass_2 = remote(place(2), place(2), send.at[4], recv.at[4], mate)
    pass_2.start()
    own.wait()
    to_mate.wait()
    pass_0.wait()
    pass_2.wait()
    to_after.wait_send()
    to_before.wait_send()


def exchange(latent, n):
    rows, d = latent.shape
    return pl.pallas_call(
        functools.partial(exchange_kernel, n),
        out_shape=jax.ShapeDtypeStruct((3, 2, rows, d), BF),
        in_specs=[VMEM],
        out_specs=VMEM,
        scratch_shapes=[
            pltpu.VMEM((rows, d), BF),
            pltpu.SemaphoreType.DMA((5,)),
            pltpu.SemaphoreType.DMA((5,)),
            pltpu.SemaphoreType.DMA,
        ],
        compiler_params=comm_params(0),
        name="node_exchange",
    )(latent)


def forward_kernel(
    count, el, ext, snd_r, rcv_r, w1, w2, gain, act_o, slope_o, normed_o, inv_o, agg_o, agg
):
    i = pl.program_id(0)
    tile, d = el.shape
    nodes = agg.shape[0]
    x_s = dot(hot_rows(column(snd_r[...]), 3 * nodes), ext[...]).astype(BF)
    x_r = dot(hot_rows(column(rcv_r[...]), nodes), ext[nodes : 2 * nodes, :]).astype(BF)
    pre = dot(el[...].astype(BF), w1[0:d, :])
    pre += dot(x_s, w1[d : 2 * d, :])
    pre += dot(x_r, w1[2 * d : 3 * d, :])
    act, slope, normed, inv = mlp_tail(pre, w2[...])
    act_o[...] = act
    slope_o[...] = slope.astype(BF)
    normed_o[...] = normed.astype(BF)
    inv_o[...] = inv
    slot = i * tile + lax.broadcasted_iota(jnp.int32, (tile, 1), 0)
    upd = jnp.where(slot < count[0], normed * gain[...], 0.0).astype(BF)
    part = dot(hot_cols(rcv_r[...], nodes), upd)

    @pl.when(i == 0)
    def _():
        agg[...] = part

    @pl.when(i > 0)
    def _():
        agg[...] += part

    @pl.when(i == pl.num_programs(0) - 1)
    def _():
        agg_o[...] = agg[...].astype(BF)


def whole(shape):
    return pl.BlockSpec(shape, lambda i: (0, 0), pipeline_mode=pl.Buffered(1))


def edge_forward(count, el, ext, snd_r, rcv_r, w1, w2, gain, tiles):
    edges, d = el.shape
    nodes = ext.shape[0] // 3
    tile = edges // tiles

    def rows(width):
        return pl.BlockSpec((tile, width), lambda i: (i, 0))

    line = pl.BlockSpec((1, tile), lambda i: (0, i))
    return pl.pallas_call(
        forward_kernel,
        grid=(tiles,),
        out_shape=(
            jax.ShapeDtypeStruct((edges, d), BF),
            jax.ShapeDtypeStruct((edges, d), BF),
            jax.ShapeDtypeStruct((edges, d), BF),
            jax.ShapeDtypeStruct((edges, 1), F32),
            jax.ShapeDtypeStruct((nodes, d), BF),
        ),
        in_specs=[
            SMEM,
            rows(d),
            whole(ext.shape),
            line,
            line,
            whole(w1.shape),
            whole(w2.shape),
            whole(gain.shape),
        ],
        out_specs=(rows(d), rows(d), rows(d), rows(1), whole((nodes, d))),
        scratch_shapes=[pltpu.VMEM((nodes, d), F32)],
        compiler_params=pltpu.CompilerParams(
            dimension_semantics=("arbitrary",), vmem_limit_bytes=LIMIT
        ),
        name="edge_forward",
    )(count, el, ext, snd_r, rcv_r, w1, w2, gain)


def node_kernel(
    agg, lat, cot, w1, w2, gain, gagg_o, part_o, dw1_o, dw2_o, other, mine, send, recv, local
):
    p, g = lax.axis_index("patch"), lax.axis_index("grp")
    mate = (p, 1 - g)
    d = lat.shape[1]
    greet([mate])
    swap = remote(agg.at[1 - g], other, send.at[0], recv.at[0], mate)
    swap.start()
    lat_bf = lat[...].astype(BF)
    pre = dot(lat_bf, w1[0:d, :])
    swap.wait()
    agg_bf = (agg[g].astype(F32) + other[...].astype(F32)).astype(BF)
    pre += dot(agg_bf, w1[d : 2 * d, :])
    act, slope, normed, inv = mlp_tail(pre, w2[...])
    gout = norm_backward(cot[...], gain[...], normed, inv)
    gpre = (dot_nt(gout, w2[...]) * slope).astype(BF)
    mine[...] = dot_nt(gpre, w1[d : 2 * d, :]).astype(BF)
    keep = pltpu.make_async_copy(mine, gagg_o.at[g], local)
    keep.start()
    give = remote(mine, gagg_o.at[g], send.at[1], recv.at[1], mate)
    give.start()
    part_o[...] = cot[...] + dot_nt(gpre, w1[0:d, :])
    dw2_o[...] = dot_tn(act, gout).astype(BF)
    dw1_o[0:d, :] = dot_tn(lat_bf, gpre).astype(BF)
    dw1_o[d : 2 * d, :] = dot_tn(agg_bf, gpre).astype(BF)
    keep.wait()
    give.wait()


def node_layer(agg, lat, cot, w1, w2, gain):
    rows, d = lat.shape
    return pl.pallas_call(
        node_kernel,
        out_shape=(
            jax.ShapeDtypeStruct((2, rows, d), BF),
            jax.ShapeDtypeStruct((rows, d), F32),
            jax.ShapeDtypeStruct(w1.shape, BF),
            jax.ShapeDtypeStruct(w2.shape, BF),
        ),
        in_specs=[VMEM] * 6,
        out_specs=(VMEM,) * 4,
        scratch_shapes=[
            pltpu.VMEM((rows, d), BF),
            pltpu.VMEM((rows, d), BF),
            pltpu.SemaphoreType.DMA((2,)),
            pltpu.SemaphoreType.DMA((2,)),
            pltpu.SemaphoreType.DMA,
        ],
        compiler_params=comm_params(1),
        name="node_layer",
    )(agg, lat, cot, w1, w2, gain)


def backward_kernel(
    count, el, ec, act, slope, normed, inv, gagg, ext, snd_r, rcv_r, w1, w2, gain,
    grad_o, sent_o, dw1_o, dw2_o, by_s, by_r, dwe, dw2,
):
    i = pl.program_id(0)
    tile, d = el.shape
    nodes = gagg.shape[0]

    @pl.when(i == 0)
    def _():
        by_s[...] = jnp.zeros_like(by_s)
        by_r[...] = jnp.zeros_like(by_r)
        dwe[...] = jnp.zeros_like(dwe)
        dw2[...] = jnp.zeros_like(dw2)

    slot = i * tile + lax.broadcasted_iota(jnp.int32, (tile, 1), 0)
    back = dot(hot_rows(column(rcv_r[...]), nodes), gagg[...])
    gupd = jnp.where(slot < count[0], ec[...] + back, 0.0)
    gout = norm_backward(gupd, gain[...], normed[...].astype(F32), inv[...])
    gpre = (dot_nt(gout, w2[...]) * slope[...].astype(F32)).astype(BF)
    grad_o[...] = ec[...] + dot_nt(gpre, w1[0:d, :])
    dw2[...] += dot_tn(act[...], gout)
    dwe[...] += dot_tn(el[...].astype(BF), gpre)
    by_s[...] += dot(hot_cols(snd_r[...], 3 * nodes), gpre)
    by_r[...] += dot(hot_cols(rcv_r[...], nodes), gpre)

    @pl.when(i == pl.num_programs(0) - 1)
    def _():
        dw2_o[...] = dw2[...].astype(BF)
        dw1_o[0:d, :] = dwe[...].astype(BF)
        s_bf = by_s[...].astype(BF)
        r_bf = by_r[...].astype(BF)
        dw1_o[d : 2 * d, :] = dot_tn(ext[...], s_bf).astype(BF)
        dw1_o[2 * d : 3 * d, :] = dot_tn(ext[nodes : 2 * nodes, :], r_bf).astype(BF)
        spread = dot_nt(s_bf, w1[d : 2 * d, :])
        sent_o[0:nodes, :] = spread[0:nodes].astype(BF)
        kept = spread[nodes : 2 * nodes] + dot_nt(r_bf, w1[2 * d : 3 * d, :])
        sent_o[nodes : 2 * nodes, :] = kept.astype(BF)
        sent_o[2 * nodes : 3 * nodes, :] = spread[2 * nodes : 3 * nodes].astype(BF)


def edge_backward(
    count, el, ec, act, slope, normed, inv, gagg, ext, snd_r, rcv_r, w1, w2, gain, tiles
):
    edges, d = el.shape
    nodes = gagg.shape[0]
    tile = edges // tiles

    def rows(width):
        return pl.BlockSpec((tile, width), lambda i: (i, 0))

    line = pl.BlockSpec((1, tile), lambda i: (0, i))
    return pl.pallas_call(
        backward_kernel,
        grid=(tiles,),
        out_shape=(
            jax.ShapeDtypeStruct((edges, d), F32),
            jax.ShapeDtypeStruct((3 * nodes, d), BF),
            jax.ShapeDtypeStruct(w1.shape, BF),
            jax.ShapeDtypeStruct(w2.shape, BF),
        ),
        in_specs=[
            SMEM, rows(d), rows(d), rows(d), rows(d), rows(d), rows(1),
            whole(gagg.shape), whole(ext.shape), line, line,
            whole(w1.shape), whole(w2.shape), whole(gain.shape),
        ],
        out_specs=(rows(d), whole((3 * nodes, d)), whole(w1.shape), whole(w2.shape)),
        scratch_shapes=[
            pltpu.VMEM((3 * nodes, d), F32),
            pltpu.VMEM((nodes, d), F32),
            pltpu.VMEM((d, d), F32),
            pltpu.VMEM((d, d), F32),
        ],
        compiler_params=pltpu.CompilerParams(
            dimension_semantics=("arbitrary",), vmem_limit_bytes=LIMIT
        ),
        name="edge_backward",
    )(count, el, ec, act, slope, normed, inv, gagg, ext, snd_r, rcv_r, w1, w2, gain)


def plan_of(rows, sizes, order):
    steps = []
    for axis in order:
        n = sizes[axis]
        if n > 1:
            left = rows // n if rows % (16 * n) == 0 else rows
            steps.append((axis, n, rows, left))
            rows = left
    return steps


class Reducer:
    def __init__(self, n, sets, d):
        self.n, self.sets, self.d = n, sets, d
        self.sizes = axis_sizes(n)
        x, y, _ = self.sizes
        self.strides = (1, x, x * y)
        orders = ((0, 1, 2), (1, 0, 2))
        self.wide = d // 2
        self.plans = [[plan_of(size, self.sizes, o) for o in orders] for _, _, size in sets]
        self.depth = len(self.plans[0][0])
        self.slots = {}
        self.scratch = {}
        for s, (_, _, size) in enumerate(sets):
            self.scratch["in", s] = pltpu.VMEM((size, d), BF)
            self.scratch["cur", s] = pltpu.VMEM((size, d), F32)
            self.scratch["out", s] = pltpu.VMEM((size, d), BF)
            self.slots["in", s] = len(self.slots)
            for c in range(2):
                for k, (axis, m, r, left) in enumerate(self.plans[s][c]):
                    self.scratch["rx", s, c, k] = pltpu.VMEM((m - 1, left, self.wide), BF)
                    self.scratch["acc", s, c, k] = pltpu.VMEM((left, self.wide), F32)
                    self.scratch["tx", s, c, k] = pltpu.VMEM((left, self.wide), BF)
                    for step in range(1, m):
                        self.slots["sum", s, c, k, step] = len(self.slots)
                        if left < r:
                            self.slots["all", s, c, k, step] = len(self.slots)
        self.scratch["send"] = pltpu.SemaphoreType.DMA((len(self.slots),))
        self.scratch["recv"] = pltpu.SemaphoreType.DMA((len(self.slots),))

    def bind(self, parts, outs, refs):
        self.parts, self.outs = parts, outs
        self.ref = dict(zip(self.scratch, refs))
        p, g = lax.axis_index("patch"), lax.axis_index("grp")
        self.p, self.g = p, g
        nx, ny, _ = self.sizes
        self.here = (lax.rem(p, nx), lax.rem(p // nx, ny), p // (nx * ny))
        self.mate = (p, 1 - g)

    def along(self, axis, step):
        c = self.here[axis]
        t = lax.rem(c + step, self.sizes[axis])
        return t, (self.p + (t - c) * self.strides[axis], self.g)

    def peers(self):
        return [self.along(a, step)[1] for a in range(3) for step in range(1, self.sizes[a])]

    def copy(self, key, src, dst, device):
        k = self.slots[key]
        return remote(src, dst, self.ref["send"].at[k], self.ref["recv"].at[k], device)

    @staticmethod
    def window(ref, start, size, first, wide):
        if not isinstance(start, int):
            start = pl.multiple_of(start, 16)
        return ref.at[pl.ds(start, size), pl.ds(first, wide)]

    def offset(self, s, c, depth):
        at = self.sets[s][1]
        for axis, m, r, left in self.plans[s][c][:depth]:
            if left < r:
                at = at + self.here[axis] * left
        return at

    def swap(self, s):
        a, at, size = self.sets[s]
        src = self.parts[a].at[1 - self.g, pl.ds(at, size)]
        return [self.copy(("in", s), src, self.ref["in", s], self.mate)]

    def sums(self, s, k):
        made = []
        for c in range(2):
            axis, m, r, left = self.plans[s][c][k]
            base = self.ref["out", s] if k == 0 else self.ref["tx", s, c, k - 1]
            first = c * self.wide if k == 0 else 0
            for step in range(1, m):
                t, device = self.along(axis, step)
                src = self.window(base, t * left if left < r else 0, left, first, self.wide)
                dst = self.ref["rx", s, c, k].at[step - 1]
                made.append(self.copy(("sum", s, c, k, step), src, dst, device))
        return made

    def gathers(self, s, k):
        made = []
        for c in range(2):
            axis, m, r, left = self.plans[s][c][k]
            if left == r:
                continue
            out = self.outs[self.sets[s][0]]
            block = self.window(out, self.offset(s, c, k + 1), left, c * self.wide, self.wide)
            for step in range(1, m):
                made.append(self.copy(("all", s, c, k, step), block, block, self.along(axis, step)[1]))
        return made

    def begin(self, s):
        for copy in self.swap(s):
            copy.start()

    def event(self, s, k):
        depth = self.depth
        if k == 0:
            a, at, size = self.sets[s]
            for copy in self.swap(s):
                copy.wait_recv()
            total = self.parts[a][self.g, at : at + size].astype(F32) + self.ref["in", s][...].astype(F32)
            self.ref["cur", s][...] = total
            self.ref["out", s][...] = total.astype(BF)
            for copy in self.sums(s, 0):
                copy.start()
        elif k <= depth:
            k -= 1
            for copy in self.sums(s, k):
                copy.wait_recv()
            for c in range(2):
                axis, m, r, left = self.plans[s][c][k]
                mine = self.here[axis] * left if left < r else 0
                base = self.ref["cur", s] if k == 0 else self.ref["acc", s, c, k - 1]
                first = c * self.wide if k == 0 else 0
                total = self.window(base, mine, left, first, self.wide)[...]
                for step in range(m - 1):
                    total += self.ref["rx", s, c, k][step].astype(F32)
                if k < depth - 1:
                    self.ref["acc", s, c, k][...] = total
                    self.ref["tx", s, c, k][...] = total.astype(BF)
                else:
                    out = self.outs[self.sets[s][0]]
                    block = self.window(out, self.offset(s, c, depth), left, c * self.wide, self.wide)
                    block[...] = total.astype(BF)
            for copy in self.sums(s, k + 1) if k < depth - 1 else self.gathers(s, k):
                copy.start()
        else:
            k = 2 * depth - k
            for copy in self.gathers(s, k):
                copy.wait_recv()
            if k > 0:
                for copy in self.gathers(s, k - 1):
                    copy.start()

    def events(self):
        return 2 * self.depth + 1

    def drain(self):
        for s in range(len(self.sets)):
            made = self.swap(s)
            for k in range(self.depth):
                made += self.sums(s, k) + self.gathers(s, k)
            for copy in made:
                copy.wait_send()


class Homing:
    def __init__(self, n, rows, d):
        self.n = n
        self.scratch = {
            "sin": pltpu.VMEM((3, rows, d), BF),
            "home": pltpu.VMEM((2, rows, d), BF),
            "from": pltpu.VMEM((2, rows, d), BF),
            "send": pltpu.SemaphoreType.DMA((5,)),
            "recv": pltpu.SemaphoreType.DMA((5,)),
        }

    def bind(self, sent, share, refs):
        self.sent, self.share = sent, share
        self.ref = dict(zip(self.scratch, refs))
        p, self.g = lax.axis_index("patch"), lax.axis_index("grp")
        self.mate = (p, 1 - self.g)
        self.after = (lax.rem(p + 1, self.n), self.g)
        self.before = (lax.rem(p + self.n - 1, self.n), self.g)

    def peers(self):
        return [self.mate, self.after, self.before]

    def copy(self, k, src, dst, device):
        return remote(src, dst, self.ref["send"].at[k], self.ref["recv"].at[k], device)

    def swaps(self):
        return [
            self.copy(k, self.sent.at[k, 1 - self.g], self.ref["sin"].at[k], self.mate)
            for k in range(3)
        ]

    def moves(self):
        home, got = self.ref["home"], self.ref["from"]
        return [
            self.copy(3, home.at[0], got.at[0], self.before),
            self.copy(4, home.at[1], got.at[1], self.after),
        ]

    def start(self):
        for copy in self.swaps():
            copy.start()

    def turn(self):
        for copy in self.swaps():
            copy.wait_recv()
        for k in (0, 2):
            total = self.sent[k, self.g].astype(F32) + self.ref["sin"][k].astype(F32)
            self.ref["home"][k // 2] = total.astype(BF)
        for copy in self.moves():
            copy.start()
        self.share[...] = self.sent[1, self.g].astype(F32) + self.ref["sin"][1].astype(F32)

    def finish(self):
        for copy in self.moves():
            copy.wait_recv()
        self.share[...] += self.ref["from"][0].astype(F32) + self.ref["from"][1].astype(F32)

    def drain(self):
        for copy in self.swaps() + self.moves():
            copy.wait_send()


def reduce_kernel(red, hom, sent, d_n1, d_n2, d_e2, d_e1, share_o, n1_o, n2_o, e2_o, e1_o, *refs):
    cut = len(red.scratch)
    red.bind((d_n1, d_n2, d_e2, d_e1), (n1_o, n2_o, e2_o, e1_o), refs[:cut])
    hom.bind(sent, share_o, refs[cut:])
    greet(hom.peers() + red.peers())
    count = len(red.sets)
    hom.start()
    for s in range(count):
        red.begin(s)
    todo = [(SKEW * k + s, k, s) for s in range(count) for k in range(1, red.events())]
    todo += [(s - 1.5, 0, s) for s in range(count)]
    todo += [(-0.8, -1, 0), (SKEW * red.depth + 0.5, -2, 0)]
    for _, k, s in sorted(todo):
        if k == -1:
            hom.turn()
        elif k == -2:
            hom.finish()
        else:
            red.event(s, k)
    red.drain()
    hom.drain()


SKEW = 2


def reduce_all(n, sent, d_n1, d_n2, d_e2, d_e1):
    _, _, rows, d = sent.shape
    parts = (d_n1, d_n2, d_e2, d_e1)
    sets = []
    for a, part in enumerate(parts):
        at, most = 0, d_n1.shape[1]
        while at < part.shape[1]:
            size = min(most, part.shape[1] - at)
            sets.append((a, at, size))
            at += size
    red, hom = Reducer(n, sets, d), Homing(n, rows, d)
    return pl.pallas_call(
        functools.partial(reduce_kernel, red, hom),
        out_shape=[jax.ShapeDtypeStruct((rows, d), F32)]
        + [jax.ShapeDtypeStruct(part.shape[1:], BF) for part in parts],
        in_specs=[VMEM] * 5,
        out_specs=[VMEM] * 5,
        scratch_shapes=list(red.scratch.values()) + list(hom.scratch.values()),
        compiler_params=comm_params(2),
        name="reduce_all",
    )(sent, *parts)


def finish_kernel(part, share, *refs):
    half = len(refs) // 2
    refs[half][...] = part[...] + share[...]
    for src, dst in zip(refs[:half], refs[half + 1 :]):
        dst[...] = src[...].astype(F32)


def finish(part, share, sums):
    steps = 4

    def blocks(x):
        return pl.BlockSpec((x.shape[0] // steps, x.shape[1]), lambda i: (i, 0))

    return pl.pallas_call(
        finish_kernel,
        grid=(steps,),
        out_shape=[jax.ShapeDtypeStruct(x.shape, F32) for x in (part, *sums)],
        in_specs=[blocks(x) for x in (part, share, *sums)],
        out_specs=[blocks(x) for x in (part, *sums)],
        name="finish",
    )(part, share, *sums)


def local(
    node_latent,
    edge_latent,
    node_cot,
    edge_cot,
    edge_w1,
    edge_w2,
    edge_gain,
    node_w1,
    node_w2,
    node_gain,
    senders,
    receivers,
    counts,
):
    n = lax.axis_size("patch")
    rows, d = node_latent.shape
    edges = edge_latent.shape[0]
    tiles = 4
    ext = exchange(node_latent, n).reshape(6 * rows, d)
    snd_r, rcv_r = senders.reshape(1, edges), receivers.reshape(1, edges)
    e_gain, n_gain = edge_gain.reshape(1, d), node_gain.reshape(1, d)
    act, slope, normed, inv, agg = edge_forward(
        counts, edge_latent, ext, snd_r, rcv_r, edge_w1, edge_w2, e_gain, tiles
    )
    gagg, part, d_n1, d_n2 = node_layer(
        agg.reshape(2, rows, d), node_latent, node_cot, node_w1, node_w2, n_gain
    )
    edge_grad, sent, d_e1, d_e2 = edge_backward(
        counts, edge_latent, edge_cot, act, slope, normed, inv, gagg.reshape(2 * rows, d), ext,
        snd_r, rcv_r, edge_w1, edge_w2, e_gain, tiles,
    )

    def halves(x):
        return x.reshape(2, x.shape[0] // 2, d)

    share, *sums = reduce_all(
        n, sent.reshape(3, 2, rows, d), halves(d_n1), halves(d_n2), halves(d_e2), halves(d_e1)
    )
    node_grad, n1, n2, e2, e1 = finish(part, share, sums)
    return node_grad, edge_grad, e1, e2, n1, n2


def solution(mesh):
    line = P(("patch", "grp"))
    block = P(("patch", "grp"), None)
    in_specs = (block,) * 4 + (P(),) * 6 + (line,) * 3
    out_specs = (block, block) + (P("grp", None),) * 4
    return jax.shard_map(local, mesh=mesh, in_specs=in_specs, out_specs=out_specs, check_vma=False)
```

```python
import functools

import jax
import jax.numpy as jnp
from jax import lax
from jax.experimental import pallas as pl
from jax.experimental.pallas import tpu as pltpu
from jax.sharding import PartitionSpec as P

EPS = 1e-05
BF = jnp.bfloat16
F32 = jnp.float32
MESH = pl.DeviceIdType.MESH
VMEM = pl.BlockSpec(memory_space=pltpu.VMEM)
SMEM = pl.BlockSpec(memory_space=pltpu.SMEM)
LIMIT = 60 * 1024 * 1024


def axis_sizes(n):
    x = round((n / 2) ** (1 / 3))
    return (x, x, 2 * x) if 2 * x**3 == n else (1, 1, n)


def dot(a, b):
    return jnp.dot(a, b, preferred_element_type=F32)


def dot_tn(a, b):
    return lax.dot_general(a, b, (((0,), (0,)), ((), ())), preferred_element_type=F32)


def dot_nt(a, b):
    return lax.dot_general(a, b, (((1,), (1,)), ((), ())), preferred_element_type=F32)


def hot_rows(col, width):
    at = lax.broadcasted_iota(jnp.int32, (col.shape[0], width), 1)
    return jnp.where(at == col, 1.0, 0.0).astype(BF)


def hot_cols(row, height):
    at = lax.broadcasted_iota(jnp.int32, (height, row.shape[1]), 0)
    return jnp.where(at == row, 1.0, 0.0).astype(BF)


def column(row):
    return jnp.transpose(jnp.broadcast_to(row, (128, row.shape[1])))[:, 0:1]


def mean(x):
    return jnp.mean(x, axis=-1, keepdims=True)


def mlp_tail(pre, w2):
    sig = jax.nn.sigmoid(pre)
    act = (pre * sig).astype(BF)
    slope = sig * (1.0 + pre * (1.0 - sig))
    out = dot(act, w2)
    center = out - mean(out)
    inv = lax.rsqrt(mean(center * center) + EPS)
    return act, slope, center * inv, inv


def norm_backward(grad, gain, normed, inv):
    scaled = grad * gain
    return (inv * (scaled - mean(scaled) - normed * mean(scaled * normed))).astype(BF)


def greet(peers):
    barrier = pltpu.get_barrier_semaphore()
    for peer in peers:
        pl.semaphore_signal(barrier, inc=1, device_id=peer, device_id_type=MESH)
    pl.semaphore_wait(barrier, len(peers))


def remote(src, dst, send, recv, device):
    return pltpu.make_async_remote_copy(
        src_ref=src, dst_ref=dst, send_sem=send, recv_sem=recv, device_id=device, device_id_type=MESH
    )


def comm_params(ident):
    return pltpu.CompilerParams(collective_id=ident, has_side_effects=True, vmem_limit_bytes=LIMIT)


def exchange_kernel(n, lat_ref, ext_ref, x_ref, send, recv, local):
    x_ref[...] = lat_ref[...].astype(BF)
    p, g = lax.axis_index("patch"), lax.axis_index("grp")
    after, before = lax.rem(p + 1, n), lax.rem(p + n - 1, n)
    mate = (p, 1 - g)
    greet([mate, (after, g), (before, g)])

    def place(slab):
        return ext_ref.at[slab, g]

    own = pltpu.make_async_copy(x_ref, place(1), local)
    to_after = remote(x_ref, place(0), send.at[0], recv.at[0], (after, g))
    to_before = remote(x_ref, place(2), send.at[1], recv.at[1], (before, g))
    to_mate = remote(x_ref, place(1), send.at[2], recv.at[2], mate)
    to_after.start()
    to_before.start()
    to_mate.start()
    own.start()
    to_after.wait_recv()
    pass_0 = remote(place(0), place(0), send.at[3], recv.at[3], mate)
    pass_0.start()
    to_before.wait_recv()
    pass_2 = remote(place(2), place(2), send.at[4], recv.at[4], mate)
    pass_2.start()
    own.wait()
    to_mate.wait()
    pass_0.wait()
    pass_2.wait()
    to_after.wait_send()
    to_before.wait_send()


def exchange(latent, n):
    rows, d = latent.shape
    return pl.pallas_call(
        functools.partial(exchange_kernel, n),
        out_shape=jax.ShapeDtypeStruct((3, 2, rows, d), BF),
        in_specs=[VMEM],
        out_specs=VMEM,
        scratch_shapes=[
            pltpu.VMEM((rows, d), BF),
            pltpu.SemaphoreType.DMA((5,)),
            pltpu.SemaphoreType.DMA((5,)),
            pltpu.SemaphoreType.DMA,
        ],
        compiler_params=comm_params(0),
        name="node_exchange",
    )(latent)


def forward_kernel(
    count, el, ext, snd_r, rcv_r, w1, w2, gain, act_o, slope_o, normed_o, inv_o, agg_o, agg
):
    i = pl.program_id(0)
    tile, d = el.shape
    nodes = agg.shape[0]
    x_s = dot(hot_rows(column(snd_r[...]), 3 * nodes), ext[...]).astype(BF)
    x_r = dot(hot_rows(column(rcv_r[...]), nodes), ext[nodes : 2 * nodes, :]).astype(BF)
    pre = dot(el[...].astype(BF), w1[0:d, :])
    pre += dot(x_s, w1[d : 2 * d, :])
    pre += dot(x_r, w1[2 * d : 3 * d, :])
    act, slope, normed, inv = mlp_tail(pre, w2[...])
    act_o[...] = act
    slope_o[...] = slope.astype(BF)
    normed_o[...] = normed.astype(BF)
    inv_o[...] = inv
    slot = i * tile + lax.broadcasted_iota(jnp.int32, (tile, 1), 0)
    upd = jnp.where(slot < count[0], normed * gain[...], 0.0).astype(BF)
    part = dot(hot_cols(rcv_r[...], nodes), upd)

    @pl.when(i == 0)
    def _():
        agg[...] = part

    @pl.when(i > 0)
    def _():
        agg[...] += part

    @pl.when(i == pl.num_programs(0) - 1)
    def _():
        agg_o[...] = agg[...].astype(BF)


def whole(shape):
    return pl.BlockSpec(shape, lambda i: (0, 0), pipeline_mode=pl.Buffered(1))


def edge_forward(count, el, ext, snd_r, rcv_r, w1, w2, gain, tiles):
    edges, d = el.shape
    nodes = ext.shape[0] // 3
    tile = edges // tiles

    def rows(width):
        return pl.BlockSpec((tile, width), lambda i: (i, 0))

    line = pl.BlockSpec((1, tile), lambda i: (0, i))
    return pl.pallas_call(
        forward_kernel,
        grid=(tiles,),
        out_shape=(
            jax.ShapeDtypeStruct((edges, d), BF),
            jax.ShapeDtypeStruct((edges, d), BF),
            jax.ShapeDtypeStruct((edges, d), BF),
            jax.ShapeDtypeStruct((edges, 1), F32),
            jax.ShapeDtypeStruct((nodes, d), BF),
        ),
        in_specs=[
            SMEM,
            rows(d),
            whole(ext.shape),
            line,
            line,
            whole(w1.shape),
            whole(w2.shape),
            whole(gain.shape),
        ],
        out_specs=(rows(d), rows(d), rows(d), rows(1), whole((nodes, d))),
        scratch_shapes=[pltpu.VMEM((nodes, d), F32)],
        compiler_params=pltpu.CompilerParams(
            dimension_semantics=("arbitrary",), vmem_limit_bytes=LIMIT
        ),
        name="edge_forward",
    )(count, el, ext, snd_r, rcv_r, w1, w2, gain)


def node_kernel(
    agg, lat, cot, w1, w2, gain, gagg_o, part_o, dw1_o, dw2_o, other, mine, send, recv, local
):
    p, g = lax.axis_index("patch"), lax.axis_index("grp")
    mate = (p, 1 - g)
    d = lat.shape[1]
    greet([mate])
    swap = remote(agg.at[1 - g], other, send.at[0], recv.at[0], mate)
    swap.start()
    lat_bf = lat[...].astype(BF)
    pre = dot(lat_bf, w1[0:d, :])
    swap.wait()
    agg_bf = (agg[g].astype(F32) + other[...].astype(F32)).astype(BF)
    pre += dot(agg_bf, w1[d : 2 * d, :])
    act, slope, normed, inv = mlp_tail(pre, w2[...])
    gout = norm_backward(cot[...], gain[...], normed, inv)
    gpre = (dot_nt(gout, w2[...]) * slope).astype(BF)
    mine[...] = dot_nt(gpre, w1[d : 2 * d, :]).astype(BF)
    keep = pltpu.make_async_copy(mine, gagg_o.at[g], local)
    keep.start()
    give = remote(mine, gagg_o.at[g], send.at[1], recv.at[1], mate)
    give.start()
    part_o[...] = cot[...] + dot_nt(gpre, w1[0:d, :])
    dw2_o[...] = dot_tn(act, gout).astype(BF)
    dw1_o[0:d, :] = dot_tn(lat_bf, gpre).astype(BF)
    dw1_o[d : 2 * d, :] = dot_tn(agg_bf, gpre).astype(BF)
    keep.wait()
    give.wait()


def node_layer(agg, lat, cot, w1, w2, gain):
    rows, d = lat.shape
    return pl.pallas_call(
        node_kernel,
        out_shape=(
            jax.ShapeDtypeStruct((2, rows, d), BF),
            jax.ShapeDtypeStruct((rows, d), F32),
            jax.ShapeDtypeStruct(w1.shape, BF),
            jax.ShapeDtypeStruct(w2.shape, BF),
        ),
        in_specs=[VMEM] * 6,
        out_specs=(VMEM,) * 4,
        scratch_shapes=[
            pltpu.VMEM((rows, d), BF),
            pltpu.VMEM((rows, d), BF),
            pltpu.SemaphoreType.DMA((2,)),
            pltpu.SemaphoreType.DMA((2,)),
            pltpu.SemaphoreType.DMA,
        ],
        compiler_params=comm_params(1),
        name="node_layer",
    )(agg, lat, cot, w1, w2, gain)


def plan_of(rows, sizes, order):
    steps = []
    for axis in order:
        n = sizes[axis]
        if n > 1:
            left = rows // n if rows % (16 * n) == 0 else rows
            steps.append((axis, n, rows, left))
            rows = left
    return steps


class Reducer:
    def __init__(self, n, sets, d):
        self.n, self.sets, self.d = n, sets, d
        self.sizes = axis_sizes(n)
        x, y, _ = self.sizes
        self.strides = (1, x, x * y)
        orders = ((0, 1, 2), (1, 0, 2))
        self.wide = d // 2
        self.plans = [[plan_of(size, self.sizes, o) for o in orders] for _, _, size in sets]
        self.depth = len(self.plans[0][0])
        self.slots = {}
        self.scratch = {}
        for s, (_, _, size) in enumerate(sets):
            self.scratch["in", s] = pltpu.VMEM((size, d), BF)
            self.scratch["cur", s] = pltpu.VMEM((size, d), F32)
            self.scratch["out", s] = pltpu.VMEM((size, d), BF)
            self.slots["in", s] = len(self.slots)
            for c in range(2):
                for k, (axis, m, r, left) in enumerate(self.plans[s][c]):
                    self.scratch["rx", s, c, k] = pltpu.VMEM((m - 1, left, self.wide), BF)
                    self.scratch["acc", s, c, k] = pltpu.VMEM((left, self.wide), F32)
                    self.scratch["tx", s, c, k] = pltpu.VMEM((left, self.wide), BF)
                    for step in range(1, m):
                        self.slots["sum", s, c, k, step] = len(self.slots)
                        if left < r:
                            self.slots["all", s, c, k, step] = len(self.slots)
        self.scratch["send"] = pltpu.SemaphoreType.DMA((len(self.slots),))
        self.scratch["recv"] = pltpu.SemaphoreType.DMA((len(self.slots),))

    def bind(self, parts, outs, refs):
        self.parts, self.outs = parts, outs
        self.ref = dict(zip(self.scratch, refs))
        p, g = lax.axis_index("patch"), lax.axis_index("grp")
        self.p, self.g = p, g
        nx, ny, _ = self.sizes
        self.here = (lax.rem(p, nx), lax.rem(p // nx, ny), p // (nx * ny))
        self.mate = (p, 1 - g)

    def along(self, axis, step):
        c = self.here[axis]
        t = lax.rem(c + step, self.sizes[axis])
        return t, (self.p + (t - c) * self.strides[axis], self.g)

    def peers(self):
        return [self.along(a, step)[1] for a in range(3) for step in range(1, self.sizes[a])]

    def copy(self, key, src, dst, device):
        k = self.slots[key]
        return remote(src, dst, self.ref["send"].at[k], self.ref["recv"].at[k], device)

    @staticmethod
    def window(ref, start, size, first, wide):
        if not isinstance(start, int):
            start = pl.multiple_of(start, 16)
        return ref.at[pl.ds(start, size), pl.ds(first, wide)]

    def offset(self, s, c, depth):
        at = self.sets[s][1]
        for axis, m, r, left in self.plans[s][c][:depth]:
            if left < r:
                at = at + self.here[axis] * left
        return at

    def swap(self, s):
        a, at, size = self.sets[s]
        src = self.parts[a].at[1 - self.g, pl.ds(at, size)]
        return [self.copy(("in", s), src, self.ref["in", s], self.mate)]

    def sums(self, s, k):
        made = []
        for c in range(2):
            axis, m, r, left = self.plans[s][c][k]
            base = self.ref["out", s] if k == 0 else self.ref["tx", s, c, k - 1]
            first = c * self.wide if k == 0 else 0
            for step in range(1, m):
                t, device = self.along(axis, step)
                src = self.window(base, t * left if left < r else 0, left, first, self.wide)
                dst = self.ref["rx", s, c, k].at[step - 1]
                made.append(self.copy(("sum", s, c, k, step), src, dst, device))
        return made

    def gathers(self, s, k):
        made = []
        for c in range(2):
            axis, m, r, left = self.plans[s][c][k]
            if left == r:
                continue
            out = self.outs[self.sets[s][0]]
            block = self.window(out, self.offset(s, c, k + 1), left, c * self.wide, self.wide)
            for step in range(1, m):
                made.append(self.copy(("all", s, c, k, step), block, block, self.along(axis, step)[1]))
        return made

    def begin(self, s):
        for copy in self.swap(s):
            copy.start()

    def event(self, s, k):
        depth = self.depth
        if k == 0:
            a, at, size = self.sets[s]
            for copy in self.swap(s):
                copy.wait_recv()
            total = self.parts[a][self.g, at : at + size].astype(F32) + self.ref["in", s][...].astype(F32)
            self.ref["cur", s][...] = total
            self.ref["out", s][...] = total.astype(BF)
            for copy in self.sums(s, 0):
                copy.start()
        elif k <= depth:
            k -= 1
            for copy in self.sums(s, k):
                copy.wait_recv()
            for c in range(2):
                axis, m, r, left = self.plans[s][c][k]
                mine = self.here[axis] * left if left < r else 0
                base = self.ref["cur", s] if k == 0 else self.ref["acc", s, c, k - 1]
                first = c * self.wide if k == 0 else 0
                total = self.window(base, mine, left, first, self.wide)[...]
                for step in range(m - 1):
                    total += self.ref["rx", s, c, k][step].astype(F32)
                if k < depth - 1:
                    self.ref["acc", s, c, k][...] = total
                    self.ref["tx", s, c, k][...] = total.astype(BF)
                else:
                    out = self.outs[self.sets[s][0]]
                    block = self.window(out, self.offset(s, c, depth), left, c * self.wide, self.wide)
                    block[...] = total.astype(BF)
            for copy in self.sums(s, k + 1) if k < depth - 1 else self.gathers(s, k):
                copy.start()
        else:
            k = 2 * depth - k
            for copy in self.gathers(s, k):
                copy.wait_recv()
            if k > 0:
                for copy in self.gathers(s, k - 1):
                    copy.start()

    def events(self):
        return 2 * self.depth + 1

    def drain(self):
        for s in range(len(self.sets)):
            made = self.swap(s)
            for k in range(self.depth):
                made += self.sums(s, k) + self.gathers(s, k)
            for copy in made:
                copy.wait_send()


class Homing:
    def __init__(self, n, rows, d):
        self.n = n
        self.scratch = {
            "sin": pltpu.VMEM((3, rows, d), BF),
            "home": pltpu.VMEM((2, rows, d), BF),
            "from": pltpu.VMEM((2, rows, d), BF),
            "send": pltpu.SemaphoreType.DMA((5,)),
            "recv": pltpu.SemaphoreType.DMA((5,)),
        }

    def bind(self, sent, share, refs):
        self.sent, self.share = sent, share
        self.ref = dict(zip(self.scratch, refs))
        p, self.g = lax.axis_index("patch"), lax.axis_index("grp")
        self.mate = (p, 1 - self.g)
        self.after = (lax.rem(p + 1, self.n), self.g)
        self.before = (lax.rem(p + self.n - 1, self.n), self.g)

    def peers(self):
        return [self.mate, self.after, self.before]

    def copy(self, k, src, dst, device):
        return remote(src, dst, self.ref["send"].at[k], self.ref["recv"].at[k], device)

    def swaps(self):
        return [
            self.copy(k, self.sent.at[k, 1 - self.g], self.ref["sin"].at[k], self.mate)
            for k in range(3)
        ]

    def moves(self):
        home, got = self.ref["home"], self.ref["from"]
        return [
            self.copy(3, home.at[0], got.at[0], self.before),
            self.copy(4, home.at[1], got.at[1], self.after),
        ]

    def start(self):
        for copy in self.swaps():
            copy.start()

    def turn(self):
        for copy in self.swaps():
            copy.wait_recv()
        for k in (0, 2):
            total = self.sent[k, self.g].astype(F32) + self.ref["sin"][k].astype(F32)
            self.ref["home"][k // 2] = total.astype(BF)
        for copy in self.moves():
            copy.start()
        self.share[...] = self.sent[1, self.g].astype(F32) + self.ref["sin"][1].astype(F32)

    def finish(self):
        for copy in self.moves():
            copy.wait_recv()
        self.share[...] += self.ref["from"][0].astype(F32) + self.ref["from"][1].astype(F32)

    def drain(self):
        for copy in self.swaps() + self.moves():
            copy.wait_send()


def backward_kernel(
    red, hom, count, el, ec, act, slope, normed, inv, gagg, ext, snd_r, rcv_r, w1, w2, gain, d_n1, d_n2,
    gin_o, share_o, n1_o, n2_o, e2_o, e1_o,
    by_s, by_r, dwe, dw2, sent, d_e2, d_e1, n1_s, n2_s, e2_s, e1_s, *refs,
):
    i = pl.program_id(0)
    last = pl.num_programs(0) - 1
    tile, d = el.shape
    nodes = gagg.shape[0]
    cut = len(red.scratch)
    red.bind((d_n1, d_n2, d_e2, d_e1), (n1_s, n2_s, e2_s, e1_s), refs[:cut])
    hom.bind(sent, share_o, refs[cut:])
    early = [s for s in range(len(red.sets)) if red.sets[s][0] < 2]
    late = [s for s in range(len(red.sets)) if red.sets[s][0] >= 2]

    @pl.when(i == 0)
    def _():
        greet(hom.peers() + red.peers())
        for s in early:
            red.begin(s)
        by_s[...] = jnp.zeros_like(by_s)
        by_r[...] = jnp.zeros_like(by_r)
        dwe[...] = jnp.zeros_like(dwe)
        dw2[...] = jnp.zeros_like(dw2)

    @pl.when(i == last - 1)
    def _():
        for s in early:
            red.event(s, 0)

    slot = i * tile + lax.broadcasted_iota(jnp.int32, (tile, 1), 0)
    back = dot(hot_rows(column(rcv_r[...]), nodes), gagg[...])
    gupd = jnp.where(slot < count[0], ec[...] + back, 0.0)
    gout = norm_backward(gupd, gain[...], normed[...].astype(F32), inv[...])
    dw2[...] += dot_tn(act[...], gout)
    gpre = (dot_nt(gout, w2[...]) * slope[...].astype(F32)).astype(BF)
    by_s[...] += dot(hot_cols(snd_r[...], 3 * nodes), gpre)
    by_r[...] += dot(hot_cols(rcv_r[...], nodes), gpre)
    dwe[...] += dot_tn(el[...].astype(BF), gpre)
    gin_o[...] = dot_nt(gpre, w1[0:d, :]).astype(BF)

    @pl.when(i == last)
    def _():
        half = d_e2.shape[1]
        d_e2[0] = dw2[0:half, :].astype(BF)
        d_e2[1] = dw2[half:d, :].astype(BF)
        begun = [s for s in late if red.sets[s][0] == 2]
        for s in begun:
            red.begin(s)
        red.event(early[0], 1)
        s_bf = by_s[...].astype(BF)
        r_bf = by_r[...].astype(BF)
        rows = nodes // 2
        for k in (0, 2, 1):
            spread = dot_nt(s_bf[k * nodes : (k + 1) * nodes], w1[d : 2 * d, :])
            if k == 1:
                spread += dot_nt(r_bf, w1[2 * d : 3 * d, :])
            sent[k, 0] = spread[0:rows].astype(BF)
            sent[k, 1] = spread[rows:nodes].astype(BF)
        hom.start()
        d_e1[0, 0:d, :] = dwe[...].astype(BF)
        side = dot_tn(ext[...], s_bf).astype(BF)
        size = d_e1.shape[1]
        d_e1[0, d:size, :] = side[0 : size - d]
        d_e1[1, 0 : 2 * d - size, :] = side[size - d : d]
        d_e1[1, 2 * d - size : size, :] = dot_tn(ext[nodes : 2 * nodes, :], r_bf).astype(BF)
        for s in late:
            if s not in begun:
                red.begin(s)
        todo = [(SKEW * (k - 2) + s, k, s) for s in early for k in range(1, red.events())]
        todo += [(SKEW * k + at, k, s) for at, s in enumerate(late) for k in range(1, red.events())]
        todo += [(at - 0.5, 0, s) for at, s in enumerate(late)]
        todo += [(-0.4, -1, 0), (SKEW * 2 * red.depth, -2, 0)]
        todo.remove((SKEW * -1 + early[0], 1, early[0]))
        for _, k, s in sorted(todo):
            if k == -1:
                hom.turn()
            elif k == -2:
                hom.finish()
            else:
                red.event(s, k)
        for out, kept in ((n1_o, n1_s), (n2_o, n2_s), (e2_o, e2_s), (e1_o, e1_s)):
            out[...] = kept[...]
        red.drain()
        hom.drain()


SKEW = 2


def edge_backward(
    n, count, el, ec, act, slope, normed, inv, gagg, ext, snd_r, rcv_r, w1, w2, gain, d_n1, d_n2, tiles
):
    edges, d = el.shape
    nodes = gagg.shape[0]
    tile = edges // tiles

    def rows(width):
        return pl.BlockSpec((tile, width), lambda i: (i, 0))

    def cube(shape):
        return pl.BlockSpec(shape, lambda i: (0, 0, 0), pipeline_mode=pl.Buffered(1))

    line = pl.BlockSpec((1, tile), lambda i: (0, i))
    sizes = (d_n1.shape[1], d_n2.shape[1], w2.shape[0] // 2, w1.shape[0] // 2)
    sets = []
    for a, size in enumerate(sizes):
        at = 0
        while at < size:
            sets.append((a, at, min(d, size - at)))
            at += d
    red, hom = Reducer(n, sets, d), Homing(n, nodes // 2, d)
    return pl.pallas_call(
        functools.partial(backward_kernel, red, hom),
        grid=(tiles,),
        out_shape=[jax.ShapeDtypeStruct((edges, d), BF), jax.ShapeDtypeStruct((nodes // 2, d), F32)]
        + [jax.ShapeDtypeStruct((size, d), BF) for size in sizes],
        in_specs=[
            SMEM, rows(d), rows(d), rows(d), rows(d), rows(d), rows(1),
            whole(gagg.shape), whole(ext.shape), line, line,
            whole(w1.shape), whole(w2.shape), whole(gain.shape), cube(d_n1.shape), cube(d_n2.shape),
        ],
        out_specs=[rows(d), whole((nodes // 2, d))] + [whole((size, d)) for size in sizes],
        scratch_shapes=[
            pltpu.VMEM((3 * nodes, d), F32),
            pltpu.VMEM((nodes, d), F32),
            pltpu.VMEM((d, d), F32),
            pltpu.VMEM((d, d), F32),
            pltpu.VMEM((3, 2, nodes // 2, d), BF),
            pltpu.VMEM((2, sizes[2], d), BF),
            pltpu.VMEM((2, sizes[3], d), BF),
        ]
        + [pltpu.VMEM((size, d), BF) for size in sizes]
        + list(red.scratch.values())
        + list(hom.scratch.values()),
        compiler_params=pltpu.CompilerParams(
            dimension_semantics=("arbitrary",),
            collective_id=2,
            has_side_effects=True,
            vmem_limit_bytes=LIMIT,
        ),
        name="edge_backward",
    )(count, el, ec, act, slope, normed, inv, gagg, ext, snd_r, rcv_r, w1, w2, gain, d_n1, d_n2)


def finish_kernel(part, share, ec, gin, *refs):
    half = (len(refs) - 2) // 2
    refs[half][...] = part[...] + share[...]
    refs[half + 1][...] = ec[...] + gin[...].astype(F32)
    for src, dst in zip(refs[:half], refs[half + 2 :]):
        dst[...] = src[...].astype(F32)


def finish(part, share, ec, gin, sums):
    steps = 4

    def blocks(x):
        return pl.BlockSpec((x.shape[0] // steps, x.shape[1]), lambda i: (i, 0))

    return pl.pallas_call(
        finish_kernel,
        grid=(steps,),
        out_shape=[jax.ShapeDtypeStruct(x.shape, F32) for x in (part, ec, *sums)],
        in_specs=[blocks(x) for x in (part, share, ec, gin, *sums)],
        out_specs=[blocks(x) for x in (part, ec, *sums)],
        compiler_params=pltpu.CompilerParams(vmem_limit_bytes=LIMIT),
        name="finish",
    )(part, share, ec, gin, *sums)


def local(
    node_latent,
    edge_latent,
    node_cot,
    edge_cot,
    edge_w1,
    edge_w2,
    edge_gain,
    node_w1,
    node_w2,
    node_gain,
    senders,
    receivers,
    counts,
):
    n = lax.axis_size("patch")
    rows, d = node_latent.shape
    edges = edge_latent.shape[0]
    tiles = 4
    ext = exchange(node_latent, n).reshape(6 * rows, d)
    snd_r, rcv_r = senders.reshape(1, edges), receivers.reshape(1, edges)
    e_gain, n_gain = edge_gain.reshape(1, d), node_gain.reshape(1, d)
    act, slope, normed, inv, agg = edge_forward(
        counts, edge_latent, ext, snd_r, rcv_r, edge_w1, edge_w2, e_gain, tiles
    )
    gagg, part, d_n1, d_n2 = node_layer(
        agg.reshape(2, rows, d), node_latent, node_cot, node_w1, node_w2, n_gain
    )

    def halves(x):
        return x.reshape(2, x.shape[0] // 2, d)

    gin, share, *sums = edge_backward(
        n, counts, edge_latent, edge_cot, act, slope, normed, inv, gagg.reshape(2 * rows, d), ext,
        snd_r, rcv_r, edge_w1, edge_w2, e_gain, halves(d_n1), halves(d_n2), tiles,
    )
    node_grad, edge_grad, n1, n2, e2, e1 = finish(part, share, edge_cot, gin, sums)
    return node_grad, edge_grad, e1, e2, n1, n2


def solution(mesh):
    line = P(("patch", "grp"))
    block = P(("patch", "grp"), None)
    in_specs = (block,) * 4 + (P(),) * 6 + (line,) * 3
    out_specs = (block, block) + (P("grp", None),) * 4
    return jax.shard_map(local, mesh=mesh, in_specs=in_specs, out_specs=out_specs, check_vma=False)
```

```python
import functools

import jax
import jax.numpy as jnp
from jax import lax
from jax.experimental import pallas as pl
from jax.experimental.pallas import tpu as pltpu
from jax.sharding import PartitionSpec as P

EPS = 1e-05
BF = jnp.bfloat16
F32 = jnp.float32
MESH = pl.DeviceIdType.MESH
VMEM = pl.BlockSpec(memory_space=pltpu.VMEM)
SMEM = pl.BlockSpec(memory_space=pltpu.SMEM)
LIMIT = 60 * 1024 * 1024


def axis_sizes(n):
    x = round((n / 2) ** (1 / 3))
    return (x, x, 2 * x) if 2 * x**3 == n else (1, 1, n)


def dot(a, b):
    return jnp.dot(a, b, preferred_element_type=F32)


def dot_tn(a, b):
    return lax.dot_general(a, b, (((0,), (0,)), ((), ())), preferred_element_type=F32)


def dot_nt(a, b):
    return lax.dot_general(a, b, (((1,), (1,)), ((), ())), preferred_element_type=F32)


def hot_rows(col, width):
    at = lax.broadcasted_iota(jnp.int32, (col.shape[0], width), 1)
    return jnp.where(at == col, 1.0, 0.0).astype(BF)


def hot_cols(row, height):
    at = lax.broadcasted_iota(jnp.int32, (height, row.shape[1]), 0)
    return jnp.where(at == row, 1.0, 0.0).astype(BF)


def column(row):
    return jnp.transpose(jnp.broadcast_to(row, (128, row.shape[1])))[:, 0:1]


def mean(x):
    return jnp.mean(x, axis=-1, keepdims=True)


def mlp_tail(pre, w2):
    sig = jax.nn.sigmoid(pre)
    act = (pre * sig).astype(BF)
    slope = sig * (1.0 + pre * (1.0 - sig))
    out = dot(act, w2)
    center = out - mean(out)
    inv = lax.rsqrt(mean(center * center) + EPS)
    return act, slope, center * inv, inv


def norm_backward(grad, gain, normed, inv):
    scaled = grad * gain
    return (inv * (scaled - mean(scaled) - normed * mean(scaled * normed))).astype(BF)


def greet(peers):
    barrier = pltpu.get_barrier_semaphore()
    for peer in peers:
        pl.semaphore_signal(barrier, inc=1, device_id=peer, device_id_type=MESH)
    pl.semaphore_wait(barrier, len(peers))


def remote(src, dst, send, recv, device):
    return pltpu.make_async_remote_copy(
        src_ref=src, dst_ref=dst, send_sem=send, recv_sem=recv, device_id=device, device_id_type=MESH
    )


def comm_params(ident):
    return pltpu.CompilerParams(collective_id=ident, has_side_effects=True, vmem_limit_bytes=LIMIT)


def exchange_kernel(n, lat_ref, ext_ref, x_ref, send, recv, local):
    x_ref[...] = lat_ref[...].astype(BF)
    p, g = lax.axis_index("patch"), lax.axis_index("grp")
    after, before = lax.rem(p + 1, n), lax.rem(p + n - 1, n)
    mate = (p, 1 - g)
    greet([mate, (after, g), (before, g)])

    def place(slab):
        return ext_ref.at[slab, g]

    own = pltpu.make_async_copy(x_ref, place(1), local)
    to_after = remote(x_ref, place(0), send.at[0], recv.at[0], (after, g))
    to_before = remote(x_ref, place(2), send.at[1], recv.at[1], (before, g))
    to_mate = remote(x_ref, place(1), send.at[2], recv.at[2], mate)
    to_after.start()
    to_before.start()
    to_mate.start()
    own.start()
    to_after.wait_recv()
    pass_0 = remote(place(0), place(0), send.at[3], recv.at[3], mate)
    pass_0.start()
    to_before.wait_recv()
    pass_2 = remote(place(2), place(2), send.at[4], recv.at[4], mate)
    pass_2.start()
    own.wait()
    to_mate.wait()
    pass_0.wait()
    pass_2.wait()
    to_after.wait_send()
    to_before.wait_send()


def exchange(latent, n):
    rows, d = latent.shape
    return pl.pallas_call(
        functools.partial(exchange_kernel, n),
        out_shape=jax.ShapeDtypeStruct((3, 2, rows, d), BF),
        in_specs=[VMEM],
        out_specs=VMEM,
        scratch_shapes=[
            pltpu.VMEM((rows, d), BF),
            pltpu.SemaphoreType.DMA((5,)),
            pltpu.SemaphoreType.DMA((5,)),
            pltpu.SemaphoreType.DMA,
        ],
        compiler_params=comm_params(0),
        name="node_exchange",
    )(latent)


def forward_kernel(
    count, el, ext, snd_r, rcv_r, w1, w2, gain, act_o, slope_o, normed_o, inv_o, agg_o, agg
):
    i = pl.program_id(0)
    tile, d = el.shape
    nodes = agg.shape[0]
    x_s = dot(hot_rows(column(snd_r[...]), 3 * nodes), ext[...]).astype(BF)
    x_r = dot(hot_rows(column(rcv_r[...]), nodes), ext[nodes : 2 * nodes, :]).astype(BF)
    pre = dot(el[...].astype(BF), w1[0:d, :])
    pre += dot(x_s, w1[d : 2 * d, :])
    pre += dot(x_r, w1[2 * d : 3 * d, :])
    act, slope, normed, inv = mlp_tail(pre, w2[...])
    act_o[...] = act
    slope_o[...] = slope.astype(BF)
    normed_o[...] = normed.astype(BF)
    inv_o[...] = inv
    slot = i * tile + lax.broadcasted_iota(jnp.int32, (tile, 1), 0)
    upd = jnp.where(slot < count[0], normed * gain[...], 0.0).astype(BF)
    part = dot(hot_cols(rcv_r[...], nodes), upd)

    @pl.when(i == 0)
    def _():
        agg[...] = part

    @pl.when(i > 0)
    def _():
        agg[...] += part

    @pl.when(i == pl.num_programs(0) - 1)
    def _():
        agg_o[...] = agg[...].astype(BF)


def whole(shape):
    return pl.BlockSpec(shape, lambda i: (0, 0), pipeline_mode=pl.Buffered(1))


def edge_forward(count, el, ext, snd_r, rcv_r, w1, w2, gain, tiles):
    edges, d = el.shape
    nodes = ext.shape[0] // 3
    tile = edges // tiles

    def rows(width):
        return pl.BlockSpec((tile, width), lambda i: (i, 0))

    line = pl.BlockSpec((1, tile), lambda i: (0, i))
    return pl.pallas_call(
        forward_kernel,
        grid=(tiles,),
        out_shape=(
            jax.ShapeDtypeStruct((edges, d), BF),
            jax.ShapeDtypeStruct((edges, d), BF),
            jax.ShapeDtypeStruct((edges, d), BF),
            jax.ShapeDtypeStruct((edges, 1), F32),
            jax.ShapeDtypeStruct((nodes, d), BF),
        ),
        in_specs=[
            SMEM,
            rows(d),
            whole(ext.shape),
            line,
            line,
            whole(w1.shape),
            whole(w2.shape),
            whole(gain.shape),
        ],
        out_specs=(rows(d), rows(d), rows(d), rows(1), whole((nodes, d))),
        scratch_shapes=[pltpu.VMEM((nodes, d), F32)],
        compiler_params=pltpu.CompilerParams(
            dimension_semantics=("arbitrary",), vmem_limit_bytes=LIMIT
        ),
        name="edge_forward",
    )(count, el, ext, snd_r, rcv_r, w1, w2, gain)


def node_kernel(
    agg, lat, cot, w1, w2, gain, gagg_o, part_o, dw1_o, dw2_o, other, mine, send, recv, local
):
    p, g = lax.axis_index("patch"), lax.axis_index("grp")
    mate = (p, 1 - g)
    d = lat.shape[1]
    greet([mate])
    swap = remote(agg.at[1 - g], other, send.at[0], recv.at[0], mate)
    swap.start()
    lat_bf = lat[...].astype(BF)
    pre = dot(lat_bf, w1[0:d, :])
    swap.wait()
    agg_bf = (agg[g].astype(F32) + other[...].astype(F32)).astype(BF)
    pre += dot(agg_bf, w1[d : 2 * d, :])
    act, slope, normed, inv = mlp_tail(pre, w2[...])
    gout = norm_backward(cot[...], gain[...], normed, inv)
    gpre = (dot_nt(gout, w2[...]) * slope).astype(BF)
    mine[...] = dot_nt(gpre, w1[d : 2 * d, :]).astype(BF)
    keep = pltpu.make_async_copy(mine, gagg_o.at[g], local)
    keep.start()
    give = remote(mine, gagg_o.at[g], send.at[1], recv.at[1], mate)
    give.start()
    part_o[...] = cot[...] + dot_nt(gpre, w1[0:d, :])
    dw2_o[...] = dot_tn(act, gout).astype(BF)
    dw1_o[0:d, :] = dot_tn(lat_bf, gpre).astype(BF)
    dw1_o[d : 2 * d, :] = dot_tn(agg_bf, gpre).astype(BF)
    keep.wait()
    give.wait()


def node_layer(agg, lat, cot, w1, w2, gain):
    rows, d = lat.shape
    return pl.pallas_call(
        node_kernel,
        out_shape=(
            jax.ShapeDtypeStruct((2, rows, d), BF),
            jax.ShapeDtypeStruct((rows, d), F32),
            jax.ShapeDtypeStruct(w1.shape, BF),
            jax.ShapeDtypeStruct(w2.shape, BF),
        ),
        in_specs=[VMEM] * 6,
        out_specs=(VMEM,) * 4,
        scratch_shapes=[
            pltpu.VMEM((rows, d), BF),
            pltpu.VMEM((rows, d), BF),
            pltpu.SemaphoreType.DMA((2,)),
            pltpu.SemaphoreType.DMA((2,)),
            pltpu.SemaphoreType.DMA,
        ],
        compiler_params=comm_params(1),
        name="node_layer",
    )(agg, lat, cot, w1, w2, gain)


def plan_of(rows, sizes, order):
    steps = []
    for axis in order:
        n = sizes[axis]
        if n > 1:
            left = rows // n if rows % (16 * n) == 0 else rows
            steps.append((axis, n, rows, left))
            rows = left
    return steps


class Reducer:
    def __init__(self, n, sets, d):
        self.n, self.sets, self.d = n, sets, d
        self.sizes = axis_sizes(n)
        x, y, _ = self.sizes
        self.strides = (1, x, x * y)
        orders = ((0, 1, 2), (1, 0, 2))
        self.wide = d // 2
        self.plans = [[plan_of(size, self.sizes, o) for o in orders] for _, _, size in sets]
        self.depth = len(self.plans[0][0])
        self.slots = {}
        self.scratch = {}
        for s, (_, _, size) in enumerate(sets):
            self.scratch["in", s] = pltpu.VMEM((size, d), BF)
            self.scratch["cur", s] = pltpu.VMEM((size, d), F32)
            self.scratch["out", s] = pltpu.VMEM((size, d), BF)
            self.slots["in", s] = len(self.slots)
            for c in range(2):
                for k, (axis, m, r, left) in enumerate(self.plans[s][c]):
                    self.scratch["rx", s, c, k] = pltpu.VMEM((m - 1, left, self.wide), BF)
                    self.scratch["acc", s, c, k] = pltpu.VMEM((left, self.wide), F32)
                    self.scratch["tx", s, c, k] = pltpu.VMEM((left, self.wide), BF)
                    for step in range(1, m):
                        self.slots["sum", s, c, k, step] = len(self.slots)
                        if left < r:
                            self.slots["all", s, c, k, step] = len(self.slots)
        self.scratch["send"] = pltpu.SemaphoreType.DMA((len(self.slots),))
        self.scratch["recv"] = pltpu.SemaphoreType.DMA((len(self.slots),))

    def bind(self, parts, outs, refs):
        self.parts, self.outs = parts, outs
        self.ref = dict(zip(self.scratch, refs))
        p, g = lax.axis_index("patch"), lax.axis_index("grp")
        self.p, self.g = p, g
        nx, ny, _ = self.sizes
        self.here = (lax.rem(p, nx), lax.rem(p // nx, ny), p // (nx * ny))
        self.mate = (p, 1 - g)

    def along(self, axis, step):
        c = self.here[axis]
        t = lax.rem(c + step, self.sizes[axis])
        return t, (self.p + (t - c) * self.strides[axis], self.g)

    def peers(self):
        return [self.along(a, step)[1] for a in range(3) for step in range(1, self.sizes[a])]

    def copy(self, key, src, dst, device):
        k = self.slots[key]
        return remote(src, dst, self.ref["send"].at[k], self.ref["recv"].at[k], device)

    @staticmethod
    def window(ref, start, size, first, wide):
        if not isinstance(start, int):
            start = pl.multiple_of(start, 16)
        return ref.at[pl.ds(start, size), pl.ds(first, wide)]

    def offset(self, s, c, depth):
        at = self.sets[s][1]
        for axis, m, r, left in self.plans[s][c][:depth]:
            if left < r:
                at = at + self.here[axis] * left
        return at

    def swap(self, s):
        a, at, size = self.sets[s]
        src = self.parts[a].at[1 - self.g, pl.ds(at, size)]
        return [self.copy(("in", s), src, self.ref["in", s], self.mate)]

    def sums(self, s, k):
        made = []
        for c in range(2):
            axis, m, r, left = self.plans[s][c][k]
            base = self.ref["out", s] if k == 0 else self.ref["tx", s, c, k - 1]
            first = c * self.wide if k == 0 else 0
            for step in range(1, m):
                t, device = self.along(axis, step)
                src = self.window(base, t * left if left < r else 0, left, first, self.wide)
                dst = self.ref["rx", s, c, k].at[step - 1]
                made.append(self.copy(("sum", s, c, k, step), src, dst, device))
        return made

    def gathers(self, s, k):
        made = []
        for c in range(2):
            axis, m, r, left = self.plans[s][c][k]
            if left == r:
                continue
            out = self.outs[self.sets[s][0]]
            block = self.window(out, self.offset(s, c, k + 1), left, c * self.wide, self.wide)
            for step in range(1, m):
                made.append(self.copy(("all", s, c, k, step), block, block, self.along(axis, step)[1]))
        return made

    def begin(self, s):
        for copy in self.swap(s):
            copy.start()

    def event(self, s, k):
        depth = self.depth
        if k == 0:
            a, at, size = self.sets[s]
            for copy in self.swap(s):
                copy.wait_recv()
            total = self.parts[a][self.g, at : at + size].astype(F32) + self.ref["in", s][...].astype(F32)
            self.ref["cur", s][...] = total
            self.ref["out", s][...] = total.astype(BF)
            for copy in self.sums(s, 0):
                copy.start()
        elif k <= depth:
            k -= 1
            for copy in self.sums(s, k):
                copy.wait_recv()
            for c in range(2):
                axis, m, r, left = self.plans[s][c][k]
                mine = self.here[axis] * left if left < r else 0
                base = self.ref["cur", s] if k == 0 else self.ref["acc", s, c, k - 1]
                first = c * self.wide if k == 0 else 0
                total = self.window(base, mine, left, first, self.wide)[...]
                for step in range(m - 1):
                    total += self.ref["rx", s, c, k][step].astype(F32)
                if k < depth - 1:
                    self.ref["acc", s, c, k][...] = total
                    self.ref["tx", s, c, k][...] = total.astype(BF)
                else:
                    out = self.outs[self.sets[s][0]]
                    block = self.window(out, self.offset(s, c, depth), left, c * self.wide, self.wide)
                    block[...] = total.astype(BF)
            for copy in self.sums(s, k + 1) if k < depth - 1 else self.gathers(s, k):
                copy.start()
        else:
            k = 2 * depth - k
            for copy in self.gathers(s, k):
                copy.wait_recv()
            if k > 0:
                for copy in self.gathers(s, k - 1):
                    copy.start()

    def events(self):
        return 2 * self.depth + 1

    def drain(self):
        for s in range(len(self.sets)):
            made = self.swap(s)
            for k in range(self.depth):
                made += self.sums(s, k) + self.gathers(s, k)
            for copy in made:
                copy.wait_send()


class Homing:
    def __init__(self, n, rows, d):
        self.n = n
        self.scratch = {
            "sin": pltpu.VMEM((3, rows, d), BF),
            "home": pltpu.VMEM((2, rows, d), BF),
            "from": pltpu.VMEM((2, rows, d), BF),
            "send": pltpu.SemaphoreType.DMA((5,)),
            "recv": pltpu.SemaphoreType.DMA((5,)),
        }

    def bind(self, sent, share, refs):
        self.sent, self.share = sent, share
        self.ref = dict(zip(self.scratch, refs))
        p, self.g = lax.axis_index("patch"), lax.axis_index("grp")
        self.mate = (p, 1 - self.g)
        self.after = (lax.rem(p + 1, self.n), self.g)
        self.before = (lax.rem(p + self.n - 1, self.n), self.g)

    def peers(self):
        return [self.mate, self.after, self.before]

    def copy(self, k, src, dst, device):
        return remote(src, dst, self.ref["send"].at[k], self.ref["recv"].at[k], device)

    def swaps(self):
        return [
            self.copy(k, self.sent.at[k, 1 - self.g], self.ref["sin"].at[k], self.mate)
            for k in range(3)
        ]

    def moves(self):
        home, got = self.ref["home"], self.ref["from"]
        return [
            self.copy(3, home.at[0], got.at[0], self.before),
            self.copy(4, home.at[1], got.at[1], self.after),
        ]

    def start(self):
        for copy in self.swaps():
            copy.start()

    def turn(self):
        for copy in self.swaps():
            copy.wait_recv()
        for k in (0, 2):
            total = self.sent[k, self.g].astype(F32) + self.ref["sin"][k].astype(F32)
            self.ref["home"][k // 2] = total.astype(BF)
        for copy in self.moves():
            copy.start()
        self.share[...] = self.sent[1, self.g].astype(F32) + self.ref["sin"][1].astype(F32)

    def finish(self):
        for copy in self.moves():
            copy.wait_recv()
        self.share[...] += self.ref["from"][0].astype(F32) + self.ref["from"][1].astype(F32)

    def drain(self):
        for copy in self.swaps() + self.moves():
            copy.wait_send()


def backward_kernel(
    red, hom, count, el, ec, act, slope, normed, inv, gagg, ext, snd_r, rcv_r, w1, w2, gain, d_n1, d_n2,
    gin_o, share_o, n1_o, n2_o, e2_o, e1_o,
    by_s, by_r, dwe, dw2, sent, d_e2, d_e1, n1_s, n2_s, e2_s, e1_s, *refs,
):
    i = pl.program_id(0)
    last = pl.num_programs(0) - 1
    tile, d = el.shape
    nodes = gagg.shape[0]
    cut = len(red.scratch)
    red.bind((d_n1, d_n2, d_e2, d_e1), (n1_s, n2_s, e2_s, e1_s), refs[:cut])
    hom.bind(sent, share_o, refs[cut:])
    early = [s for s in range(len(red.sets)) if red.sets[s][0] < 2]
    late = [s for s in range(len(red.sets)) if red.sets[s][0] >= 2]

    @pl.when(i == 0)
    def _():
        greet(hom.peers() + red.peers())
        for s in early:
            red.begin(s)
        by_s[...] = jnp.zeros_like(by_s)
        by_r[...] = jnp.zeros_like(by_r)
        dwe[...] = jnp.zeros_like(dwe)
        dw2[...] = jnp.zeros_like(dw2)

    @pl.when(i == last - 1)
    def _():
        for s in early:
            red.event(s, 0)

    slot = i * tile + lax.broadcasted_iota(jnp.int32, (tile, 1), 0)
    back = dot(hot_rows(column(rcv_r[...]), nodes), gagg[...])
    gupd = jnp.where(slot < count[0], ec[...] + back, 0.0)
    gout = norm_backward(gupd, gain[...], normed[...].astype(F32), inv[...])
    dw2[...] += dot_tn(act[...], gout)
    gpre = (dot_nt(gout, w2[...]) * slope[...].astype(F32)).astype(BF)
    by_s[...] += dot(hot_cols(snd_r[...], 3 * nodes), gpre)
    by_r[...] += dot(hot_cols(rcv_r[...], nodes), gpre)
    dwe[...] += dot_tn(el[...].astype(BF), gpre)
    gin_o[...] = dot_nt(gpre, w1[0:d, :]).astype(BF)

    @pl.when(i == last)
    def _():
        half = d_e2.shape[1]
        d_e2[0] = dw2[0:half, :].astype(BF)
        d_e2[1] = dw2[half:d, :].astype(BF)
        begun = [s for s in late if red.sets[s][0] == 2]
        for s in begun:
            red.begin(s)
        red.event(early[0], 1)
        s_bf = by_s[...].astype(BF)
        r_bf = by_r[...].astype(BF)
        rows = nodes // 2
        for k in (0, 2, 1):
            spread = dot_nt(s_bf[k * nodes : (k + 1) * nodes], w1[d : 2 * d, :])
            if k == 1:
                spread += dot_nt(r_bf, w1[2 * d : 3 * d, :])
            sent[k, 0] = spread[0:rows].astype(BF)
            sent[k, 1] = spread[rows:nodes].astype(BF)
        hom.start()
        d_e1[0, 0:d, :] = dwe[...].astype(BF)
        side = dot_tn(ext[...], s_bf).astype(BF)
        size = d_e1.shape[1]
        d_e1[0, d:size, :] = side[0 : size - d]
        d_e1[1, 0 : 2 * d - size, :] = side[size - d : d]
        d_e1[1, 2 * d - size : size, :] = dot_tn(ext[nodes : 2 * nodes, :], r_bf).astype(BF)
        for s in late:
            if s not in begun:
                red.begin(s)
        todo = [(SKEW * (k - 2) + s, k, s) for s in early for k in range(1, red.events())]
        todo += [(SKEW * k + at, k, s) for at, s in enumerate(late) for k in range(1, red.events())]
        todo += [(at - 0.5, 0, s) for at, s in enumerate(late)]
        todo += [(-0.4, -1, 0), (SKEW * 2 * red.depth, -2, 0)]
        todo.remove((SKEW * -1 + early[0], 1, early[0]))
        for _, k, s in sorted(todo):
            if k == -1:
                hom.turn()
            elif k == -2:
                hom.finish()
            else:
                red.event(s, k)
        for out, kept in ((n1_o, n1_s), (n2_o, n2_s), (e2_o, e2_s), (e1_o, e1_s)):
            out[...] = kept[...]
        red.drain()
        hom.drain()


SKEW = 1


def edge_backward(
    n, count, el, ec, act, slope, normed, inv, gagg, ext, snd_r, rcv_r, w1, w2, gain, d_n1, d_n2, tiles
):
    edges, d = el.shape
    nodes = gagg.shape[0]
    tile = edges // tiles

    def rows(width):
        return pl.BlockSpec((tile, width), lambda i: (i, 0))

    def cube(shape):
        return pl.BlockSpec(shape, lambda i: (0, 0, 0), pipeline_mode=pl.Buffered(1))

    line = pl.BlockSpec((1, tile), lambda i: (0, i))
    sizes = (d_n1.shape[1], d_n2.shape[1], w2.shape[0] // 2, w1.shape[0] // 2)
    sets = []
    for a, size in enumerate(sizes):
        at = 0
        while at < size:
            sets.append((a, at, min(d, size - at)))
            at += d
    red, hom = Reducer(n, sets, d), Homing(n, nodes // 2, d)
    return pl.pallas_call(
        functools.partial(backward_kernel, red, hom),
        grid=(tiles,),
        out_shape=[jax.ShapeDtypeStruct((edges, d), BF), jax.ShapeDtypeStruct((nodes // 2, d), F32)]
        + [jax.ShapeDtypeStruct((size, d), BF) for size in sizes],
        in_specs=[
            SMEM, rows(d), rows(d), rows(d), rows(d), rows(d), rows(1),
            whole(gagg.shape), whole(ext.shape), line, line,
            whole(w1.shape), whole(w2.shape), whole(gain.shape), cube(d_n1.shape), cube(d_n2.shape),
        ],
        out_specs=[rows(d), whole((nodes // 2, d))] + [whole((size, d)) for size in sizes],
        scratch_shapes=[
            pltpu.VMEM((3 * nodes, d), F32),
            pltpu.VMEM((nodes, d), F32),
            pltpu.VMEM((d, d), F32),
            pltpu.VMEM((d, d), F32),
            pltpu.VMEM((3, 2, nodes // 2, d), BF),
            pltpu.VMEM((2, sizes[2], d), BF),
            pltpu.VMEM((2, sizes[3], d), BF),
        ]
        + [pltpu.VMEM((size, d), BF) for size in sizes]
        + list(red.scratch.values())
        + list(hom.scratch.values()),
        compiler_params=pltpu.CompilerParams(
            dimension_semantics=("arbitrary",),
            collective_id=2,
            has_side_effects=True,
            vmem_limit_bytes=LIMIT,
        ),
        name="edge_backward",
    )(count, el, ec, act, slope, normed, inv, gagg, ext, snd_r, rcv_r, w1, w2, gain, d_n1, d_n2)


def finish_kernel(part, share, ec, gin, *refs):
    half = (len(refs) - 2) // 2
    refs[half][...] = part[...] + share[...]
    refs[half + 1][...] = ec[...] + gin[...].astype(F32)
    for src, dst in zip(refs[:half], refs[half + 2 :]):
        dst[...] = src[...].astype(F32)


def finish(part, share, ec, gin, sums):
    steps = 4

    def blocks(x):
        return pl.BlockSpec((x.shape[0] // steps, x.shape[1]), lambda i: (i, 0))

    return pl.pallas_call(
        finish_kernel,
        grid=(steps,),
        out_shape=[jax.ShapeDtypeStruct(x.shape, F32) for x in (part, ec, *sums)],
        in_specs=[blocks(x) for x in (part, share, ec, gin, *sums)],
        out_specs=[blocks(x) for x in (part, ec, *sums)],
        compiler_params=pltpu.CompilerParams(vmem_limit_bytes=LIMIT),
        name="finish",
    )(part, share, ec, gin, *sums)


def local(
    node_latent,
    edge_latent,
    node_cot,
    edge_cot,
    edge_w1,
    edge_w2,
    edge_gain,
    node_w1,
    node_w2,
    node_gain,
    senders,
    receivers,
    counts,
):
    n = lax.axis_size("patch")
    rows, d = node_latent.shape
    edges = edge_latent.shape[0]
    tiles = 4
    ext = exchange(node_latent, n).reshape(6 * rows, d)
    snd_r, rcv_r = senders.reshape(1, edges), receivers.reshape(1, edges)
    e_gain, n_gain = edge_gain.reshape(1, d), node_gain.reshape(1, d)
    act, slope, normed, inv, agg = edge_forward(
        counts, edge_latent, ext, snd_r, rcv_r, edge_w1, edge_w2, e_gain, tiles
    )
    gagg, part, d_n1, d_n2 = node_layer(
        agg.reshape(2, rows, d), node_latent, node_cot, node_w1, node_w2, n_gain
    )

    def halves(x):
        return x.reshape(2, x.shape[0] // 2, d)

    gin, share, *sums = edge_backward(
        n, counts, edge_latent, edge_cot, act, slope, normed, inv, gagg.reshape(2 * rows, d), ext,
        snd_r, rcv_r, edge_w1, edge_w2, e_gain, halves(d_n1), halves(d_n2), tiles,
    )
    node_grad, edge_grad, n1, n2, e2, e1 = finish(part, share, edge_cot, gin, sums)
    return node_grad, edge_grad, e1, e2, n1, n2


def solution(mesh):
    line = P(("patch", "grp"))
    block = P(("patch", "grp"), None)
    in_specs = (block,) * 4 + (P(),) * 6 + (line,) * 3
    out_specs = (block, block) + (P("grp", None),) * 4
    return jax.shard_map(local, mesh=mesh, in_specs=in_specs, out_specs=out_specs, check_vma=False)
```
